256 devices in a mesh: pitch: 16 (over x_lo, z), radial: 8 (over y, core), axial: 2 (over x_hi).
Axes of the slice: x: 4 (x_hi: 2, x_lo: 2; x = x_hi * 2 + x_lo), y: 4, z: 8, core: 2. Of those that a mesh axis runs over, the one named last changes fastest.
Arguments:
- density: float32 [9, 4, 64, 2048], P(None, 'axial', 'radial', 'pitch'), may hold values from 0.5 to 2
- moments: float32 [9, 4, 4, 64, 2048], P(None, None, 'axial', 'radial', 'pitch'), may hold values from -6 to 6
- shifts: int32 [9], replicated, may hold values from 0 to 2047, as said below
Outputs:
- residual: float32 [9, 5, 4, 64, 2048], P(None, None, 'axial', 'radial', 'pitch')
- update: float32 [9, 5, 4, 64, 2048], P(None, None, 'axial', 'radial', 'pitch')
The draws below stay inside these ranges and needn't reach their ends.
Inputs may be any that keep to these rules, and one draw needn't show every extreme that they name: `shifts`: every instance's offset lies in 0 to 2047 and some instance has offset 2048 - 1.
All inputs are finite; a program needn't handle non-finite values.
Results may differ from the reference program's by a relative error of at most 0.0005.
Values sent between devices are 32-bit elements; how exact they have to be, the bound alone decides.
No kernel may reach another device: no remote copies, remote signals or barrier semaphores. Data moves between devices by JAX's collectives and lax.ppermute only.
A program may use at most 192 MiB of HBM per device.

```python
import math
import jax
import jax.numpy as jnp
import numpy as np
from jax import lax

INST = 9
A_DEV = 2
NPITCH = 2048
NRAD = 64
NAX = 4


def draw_shifts(key, part):
    drawn = jax.random.randint(jax.random.fold_in(key, 11), (INST,), 0, NPITCH)
    picked = jax.random.randint(jax.random.fold_in(key, 12), (), 0, INST)
    return jnp.where(jnp.arange(INST) == picked, NPITCH - 1, drawn).astype(jnp.int32)


def shard_levels(stream_key, shape, shards, least, largest):
    level = 1.0
    for dim, blocks in shards:
        draws = jax.random.uniform(jax.random.fold_in(jax.random.fold_in(stream_key, 6), dim), (blocks,), jnp.float32, least / len(shards), largest / len(shards))
        level = level * jnp.repeat(jnp.exp(draws), shape[dim] // blocks).reshape((-1,) + (1,) * (len(shape) - 1 - dim))
    return level


def centred(stream_key, shape, scale, most, split=(), kind=jnp.bfloat16):
    gain = shard_levels(stream_key, shape, split, -0.22, 0.18) if split else 1.0
    values = jax.random.normal(stream_key, shape, jnp.float32) * scale * gain
    return jnp.minimum(jnp.maximum(values, -most), most).astype(kind)


def setup_inputs(seed: int = 0) -> dict:
    arg_keys = jax.random.split(jax.random.key(seed), 4)
    return {
        "density": jnp.clip(jnp.exp(math.log(2.0) - 1.3862944 * jax.random.uniform(arg_keys[0], (INST, NAX, NRAD, NPITCH), jnp.float32) ** shard_levels(arg_keys[0], (INST, NAX, NRAD, NPITCH), ((1, 2), (2, 8), (3, 16)), -0.2, 0.2)), 0.5, 2.0),
        "moments": centred(arg_keys[1], (INST, 4, NAX, NRAD, NPITCH), 1.0, 6.0, ((2, 2), (3, 8), (4, 16)), jnp.float32),
        "shifts": draw_shifts(jax.random.fold_in(arg_keys[3], 71), 0),
    }


COEFFS = (0.75, -0.15, 1.0 / 60.0)
GAMMA_LESS = 0.4


def spectral_table(count):
    points = np.arange(count)
    spread = points[:, None] - points[None, :]
    nonzero = np.where(spread == 0, 1, spread)
    entries = 0.5 * np.where(spread % 2 == 0, 1.0, -1.0) / np.sin(np.pi * nonzero / count)
    return jnp.asarray(np.where(spread == 0, 0.0, entries), jnp.float32)


def fluxes(density, moments):
    axial_m = moments[:, 0]
    radial_m = moments[:, 1]
    pitch_m = moments[:, 2]
    energy = moments[:, 3]
    pressure = GAMMA_LESS * (energy - 0.5 * (axial_m * axial_m + radial_m * radial_m + pitch_m * pitch_m) / density)
    pitch_v = pitch_m / density
    radial_v = radial_m / density
    along_pitch = jnp.stack([pitch_m, axial_m * pitch_v, radial_m * pitch_v, pitch_m * pitch_v + pressure, (energy + pressure) * pitch_v], axis=1)
    along_radial = jnp.stack([radial_m, axial_m * radial_v, radial_m * radial_v + pressure, pitch_m * radial_v, (energy + pressure) * radial_v], axis=1)
    return along_pitch, along_radial


def reference(density, moments, shifts):
    fields = jnp.concatenate([density[:, None], moments], axis=1)
    along_pitch, along_radial = fluxes(density, moments)
    deriv_p = jnp.zeros_like(fields)
    for offset, weight in enumerate(COEFFS):
        reach = offset + 1
        deriv_p = deriv_p + weight * (jnp.roll(along_pitch, -reach, axis=4) - jnp.roll(along_pitch, reach, axis=4))
    padded = jnp.pad(along_radial, ((0, 0), (0, 0), (0, 0), (3, 3), (0, 0)))
    deriv_r = jnp.zeros_like(fields)
    for offset, weight in enumerate(COEFFS):
        reach = offset + 1
        deriv_r = deriv_r + weight * (padded[:, :, :, 3 + reach:3 + reach + NRAD] - padded[:, :, :, 3 - reach:3 - reach + NRAD])
    spectral = jnp.einsum("nm,mvarp->nvarp", spectral_table(INST), fields, precision=lax.Precision.HIGHEST)
    rotor = fields[:, :, A_DEV - 1]
    stator = fields[:, :, A_DEV]
    columns = jnp.arange(NPITCH, dtype=jnp.int32)
    to_stator_idx = (columns[None, :] - shifts[:, None]) % NPITCH
    to_rotor_idx = (columns[None, :] + shifts[:, None]) % NPITCH
    to_stator = jnp.take_along_axis(rotor, to_stator_idx[:, None, None, :], axis=3)
    to_rotor = jnp.take_along_axis(stator, to_rotor_idx[:, None, None, :], axis=3)
    residual = deriv_p + deriv_r + spectral
    residual = residual.at[:, :, A_DEV - 1].add(to_rotor - rotor)
    residual = residual.at[:, :, A_DEV].add(to_stator - stator)
    smooth_eps = float(NPITCH * NPITCH // 16)
    modes = jnp.arange(NPITCH).astype(jnp.float32)
    eigen = 1.0 + 2.0 * smooth_eps - 2.0 * smooth_eps * jnp.cos(2.0 * np.pi * modes / NPITCH)
    update = jnp.real(jnp.fft.ifft(jnp.fft.fft(residual, axis=-1) / eigen, axis=-1)).astype(jnp.float32)
    return residual, update
```

```python
import math

import jax
import jax.numpy as jnp
import numpy as np
from jax import lax
from jax.experimental import pallas as pl
from jax.experimental.pallas import tpu as pltpu
from jax.sharding import PartitionSpec as P

COEFFS = (0.75, -0.15, 1.0 / 60.0)
GAMMA_LESS = 0.4
HIGHEST = lax.Precision.HIGHEST

INST = 9
VARS = 5
PLANES = 2
ROWS = 8
WIDTH = 128
RING = 16
PAIRS = INST * VARS
PIECE = 3
SLOTS = RING * PIECE
LANES = SLOTS * ROWS
SENT = 40


def spectral_weights():
    return [0.5 * (-1.0) ** k / math.sin(math.pi * k / INST) for k in range(1, INST // 2 + 1)]


def tables():
    extent = WIDTH * RING
    eps = float(extent * extent // 16)
    rho = 2.0 * eps / (1.0 + 2.0 * eps + math.sqrt(1.0 + 4.0 * eps))
    gain = rho / (eps * (1.0 - rho * rho))
    lam = rho**WIDTH
    closing = 1.0 / (1.0 - lam**RING)
    at = np.arange(WIDTH)
    reach = np.zeros((WIDTH, WIDTH + 6))
    for k, weight in enumerate(COEFFS, 1):
        reach[at, at - k + 3] += weight
        reach[at, at + k + 3] -= weight
    spots = np.arange(-3, WIDTH + 3)
    green = gain * rho ** np.abs(at[:, None] - at[None, :])
    wide = gain * rho ** np.abs(spots[:, None] - at[None, :])
    local = np.concatenate([reach[:, 3:-3], reach @ wide, green], axis=1)
    rise = rho ** (WIDTH - 1.0 - at)
    fall = rho ** (at + 0.0)
    kappa = sum(weight * (rho**k - rho**-k) for k, weight in enumerate(COEFFS, 1))
    pick = np.zeros((16, WIDTH))
    pick[0:3, 0:3] = np.eye(3)
    pick[3:6, WIDTH - 3 :] = np.eye(3)
    pick[6] = kappa * rise
    pick[7] = -kappa * fall
    pick[8 + 6] = rise
    pick[8 + 7] = fall
    side = np.zeros((24, 2 * WIDTH))
    for c in range(3):
        for m in range(3):
            if 1 <= 3 + m - c <= 3:
                w = -COEFFS[3 + m - c - 1]
                side[3 + c, m] += w
                side[3 + c, WIDTH:] += w * gain * (rho ** np.abs(at - m) - rho ** (at - m + 0.0))
            if c + 1 + m <= 3:
                w = COEFFS[c + m]
                spot = WIDTH - 1 - m
                side[8 + c, spot] += w
                side[8 + c, WIDTH:] += w * gain * (
                    rho ** np.abs(at - spot) - rho ** (spot - at + 0.0)
                )
    side[16, WIDTH:] = gain * rho ** (at + 1.0)
    side[17, WIDTH:] = gain * rho ** (WIDTH - at + 0.0)
    sums = np.zeros((WIDTH, WIDTH))
    sums[:, 0:RING] = rise[:, None]
    sums[:, RING : 2 * RING] = fall[:, None]
    ring = np.arange(RING)
    powers = np.zeros((RING, WIDTH))
    powers[:, 0:RING] = closing * lam ** ((ring[None, :] - ring[:, None] - 1) % RING)
    powers[:, RING : 2 * RING] = closing * lam ** ((ring[:, None] - ring[None, :] - 1) % RING)
    return [np.asarray(t, np.float32) for t in (local, pick, side, sums, powers)]


def field(density, moments, v, a):
    return density[:, a] if v == 0 else moments[:, v - 1, a]


def dot(a, b, contract):
    return lax.dot_general(
        a, b, (contract, ((), ())), precision=HIGHEST, preferred_element_type=jnp.float32
    )


def row_index(shape):
    return lax.broadcasted_iota(jnp.int32, shape, len(shape) - 2)


def pack_kernel(density, moments, facing, first, last):
    axial = lax.axis_index("axial")
    base = (1 - axial) * RING
    low = row_index((INST, ROWS, WIDTH)) < 4
    for v in range(VARS):
        one, two = field(density, moments, v, 0), field(density, moments, v, 1)
        edge = jnp.where(axial == 0, two, one)
        heads = jnp.where(low, one, pltpu.roll(two, 4, 1))
        tails = jnp.where(low, pltpu.roll(one, 4, 1), two)
        for n in range(INST):
            pair = n * VARS + v
            facing[base + pair // PIECE, pair % PIECE] = edge[n]
            first[pair] = heads[n]
            last[pair] = tails[n]
    zero = jnp.zeros((ROWS, WIDTH), jnp.float32)
    for pair in range(PAIRS, SLOTS):
        facing[base + pair // PIECE, pair % PIECE] = zero


def fluxes(d, ma, mr, mp, e, both):
    inverse = 1.0 / d
    pressure = GAMMA_LESS * (e - 0.5 * (ma * ma + mr * mr + mp * mp) * inverse)
    vr = mr * inverse
    total = e + pressure
    radial = (mr, ma * vr, mr * vr + pressure, mp * vr, total * vr)
    if not both:
        return radial
    wp = mp * inverse
    return (mp, ma * wp, mr * wp, mp * wp + pressure, total * wp), radial


def main_kernel(density, moments, above, below, local, pick, res, upd, cols, sums, flux, rest):
    axial = lax.axis_index("axial")
    radial = lax.axis_index("radial")
    shape = (INST, ROWS, WIDTH)
    row = row_index(shape)
    low = row < 4
    known = jnp.where(low, (radial < lax.axis_size("radial") - 1).astype(jnp.int32), (radial > 0).astype(jnp.int32)) > 0
    weights = spectral_weights()
    zero = jnp.zeros((ROWS, WIDTH), jnp.float32)
    for a in range(PLANES):
        fields = [field(density, moments, v, a) for v in range(VARS)]
        rims = []
        for v in range(VARS):
            up = jnp.stack([above[n * VARS + v] for n in range(INST)])
            down = jnp.stack([below[n * VARS + v] for n in range(INST)])
            if a == 0:
                rims.append(jnp.where(low, up, pltpu.roll(down, 4, 1)))
            else:
                rims.append(jnp.where(low, pltpu.roll(up, 4, 1), down))
        along_pitch, along_radial = fluxes(*fields, True)
        beyond = fluxes(*rims, False)
        mask = jnp.where(axial == 0, a == PLANES - 1, a == 0).astype(jnp.float32)
        for v in range(VARS):
            own, rim = along_radial[v], jnp.where(known, beyond[v], 0.0)
            total = -mask * fields[v]
            for k, weight in enumerate(COEFFS, 1):
                ahead = pltpu.roll(jnp.where(row >= k, own, rim), ROWS - k, 1)
                behind = pltpu.roll(jnp.where(row < ROWS - k, own, rim), k, 1)
                total = total + weight * (ahead - behind)
            f = fields[v]
            for k, weight in enumerate(weights, 1):
                back = jnp.concatenate([f[INST - k :], f[: INST - k]], axis=0)
                forth = jnp.concatenate([f[k:], f[:k]], axis=0)
                total = total + weight * (back - forth)
            for n in range(INST):
                at = (a * SLOTS + n * VARS + v) * ROWS
                rest[at : at + ROWS] = total[n]
                flux[at : at + ROWS] = along_pitch[v][n]
        for pair in range(PAIRS, SLOTS):
            at = (a * SLOTS + pair) * ROWS
            rest[at : at + ROWS] = zero
            flux[at : at + ROWS] = zero
    through = dot(flux[...], local[:, 0 : 2 * WIDTH], ((1,), (0,)))
    res[...] = rest[...] + through[:, 0:WIDTH]
    upd[...] = through[:, WIDTH:] + dot(rest[...], local[:, 2 * WIDTH :], ((1,), (0,)))
    edge = dot(pick[0:8], flux[...], ((1,), (1,)))
    cols[...] = edge
    sums[...] = edge + dot(pick[8:16], rest[...], ((1,), (1,)))


def align_kernel(shifts, whole, sums, weigh, powers, out, rolled):
    axial = lax.axis_index("axial")
    place = lax.axis_index("pitch")
    extent = WIDTH * RING
    base = (1 - axial) * RING
    lane = lax.broadcasted_iota(jnp.int32, (ROWS, WIDTH), 1)
    for j in range(PIECE):
        inst = jnp.minimum((place * PIECE + j) // VARS, INST - 1)
        shift = shifts[inst]
        offset = jnp.where(axial == 1, shift, (extent - shift) & (extent - 1))
        blocks, within = offset >> 7, offset & (WIDTH - 1)
        turned = pltpu.roll(whole[pl.ds(base, RING), j], within, 2)
        rolled[0:RING] = turned
        rolled[RING : 2 * RING] = turned
        for d in range(RING):
            here = rolled[RING + d - blocks]
            before = rolled[RING - 1 + d - blocks]
            at = d * SENT + j * ROWS
            out[at : at + ROWS] = jnp.where(lane < within, before, here)
    tall = PIECE * ROWS
    carried = jnp.zeros((tall, WIDTH), jnp.float32)
    for d in range(RING):
        block = out[d * SENT : d * SENT + tall]
        carried = carried + dot(block, weigh[...], ((1,), (0,))) * powers[d : d + 1]
    spread = powers[pl.ds(place, 1)]
    column = lax.broadcasted_iota(jnp.int32, (8, WIDTH), 1)
    line = row_index((8, WIDTH))
    extra = jnp.where(
        line == 0,
        jnp.where(column < RING, spread, 0.0),
        jnp.where((line == 1) & (column >= RING), spread, 0.0),
    )
    left = jnp.concatenate([carried, extra], axis=0)
    target = (1 - axial) * LANES + place * tall
    spots = lax.broadcasted_iota(jnp.int32, (tall, 2 * LANES), 1)
    select = (spots == target + row_index((tall, 2 * LANES))).astype(jnp.float32)
    totals = pltpu.roll(sums[...], 2, 0)
    right = jnp.concatenate([select, totals], axis=0)
    carries = dot(left, right, ((0,), (0,)))
    for t in range(6):
        at = slice(t * WIDTH, (t + 1) * WIDTH)
        out[pl.ds(tall + t, RING, SENT)] = carries[0:RING, at]
        out[pl.ds(tall + 6 + t, RING, SENT)] = carries[RING : 2 * RING, at]


def final_kernel(res, upd, got, left, right, local, side, residual, update):
    axial = lax.axis_index("axial")
    tall = PIECE * ROWS
    windows = got[:, 0:tall].reshape(LANES, WIDTH)
    smoothed = dot(windows, local[:, 2 * WIDTH :], ((1,), (0,)))
    carries = jnp.sum(got[:, tall:SENT], axis=0)
    line = row_index((8, WIDTH))
    for t in range(6):
        a, part = t // 3, t % 3
        at = slice(t * WIDTH, (t + 1) * WIDTH)
        pair = jnp.where(
            line == 0, carries[t : t + 1], jnp.where(line == 1, carries[6 + t : 7 + t], 0.0)
        )
        sides = jnp.concatenate([left[:, at], right[:, at], pair], axis=0)
        added = dot(sides, side[...], ((0,), (0,)))
        mine = axial == 1 - a
        here = slice(part * WIDTH, (part + 1) * WIDTH)
        r = res[at] + added[:, 0:WIDTH] + jnp.where(mine, windows[here], 0.0)
        u = upd[at] + added[:, WIDTH:] + jnp.where(mine, smoothed[here], 0.0)
        for j in range(16):
            pair_at = part * 16 + j
            if pair_at < PAIRS:
                n, v = pair_at // VARS, pair_at % VARS
                residual[n, v, a] = r[j * ROWS : (j + 1) * ROWS]
                update[n, v, a] = u[j * ROWS : (j + 1) * ROWS]


def call(kernel, outs, scratch=(), scalars=0, work=(0, 0), inputs=0):
    vmem = pl.BlockSpec(memory_space=pltpu.VMEM)
    smem = pl.BlockSpec(memory_space=pltpu.SMEM)
    return pl.pallas_call(
        kernel,
        out_shape=[jax.ShapeDtypeStruct(s, jnp.float32) for s in outs],
        in_specs=[smem] * scalars + [vmem] * inputs,
        out_specs=[vmem] * len(outs),
        scratch_shapes=[pltpu.VMEM(s, jnp.float32) for s in scratch],
        cost_estimate=pl.CostEstimate(flops=work[0], bytes_accessed=work[1], transcendentals=0),
    )


def local_step(density, moments, shifts):
    local, pick, side, weigh, powers = [jnp.asarray(t) for t in tables()]
    height = PLANES * LANES
    facing, first, last = call(
        pack_kernel,
        [(2 * RING, PIECE, ROWS, WIDTH), (PAIRS, ROWS, WIDTH), (PAIRS, ROWS, WIDTH)],
        inputs=2,
        work=(10**6, 10**6),
    )(density, moments)
    whole = lax.all_to_all(facing, ("axial", "pitch"), 0, 0)
    count_r = lax.axis_size("radial")
    up = [(i, i + 1) for i in range(count_r - 1)]
    down = [(j, i) for i, j in up]
    above = lax.ppermute(first, "radial", down)
    below = lax.ppermute(last, "radial", up)
    res, upd, cols, sums = call(
        main_kernel,
        [(height, WIDTH), (height, WIDTH), (8, height), (8, height)],
        scratch=[(height, WIDTH), (height, WIDTH)],
        inputs=6,
        work=(10**8, 2 * 10**6),
    )(density, moments, above, below, local, pick)
    ring = [(i, (i + 1) % RING) for i in range(RING)]
    back = [(j, i) for i, j in ring]
    left = lax.ppermute(cols, "pitch", ring)
    right = lax.ppermute(cols, "pitch", back)
    (send,) = call(
        align_kernel,
        [(RING * SENT, WIDTH)],
        scratch=[(2 * RING, ROWS, WIDTH)],
        scalars=1,
        inputs=4,
        work=(10**7, 10**6),
    )(shifts, whole, sums, weigh, powers)
    got = lax.all_to_all(send.reshape(RING, SENT, WIDTH), "pitch", 0, 0)
    shape = (INST, VARS, PLANES, ROWS, WIDTH)
    return tuple(
        call(final_kernel, [shape, shape], inputs=7, work=(10**7, 2 * 10**6))(
            res, upd, got, left, right, local, side
        )
    )


def solution(mesh):
    in_specs = (P(None, "axial", "radial", "pitch"), P(None, None, "axial", "radial", "pitch"), P())
    out_specs = (
        P(None, None, "axial", "radial", "pitch"),
        P(None, None, "axial", "radial", "pitch"),
    )
    return jax.shard_map(
        local_step, mesh=mesh, in_specs=in_specs, out_specs=out_specs, check_vma=False
    )
```

```python
import math

import jax
import jax.numpy as jnp
import numpy as np
from jax import lax
from jax.experimental import pallas as pl
from jax.experimental.pallas import tpu as pltpu
from jax.sharding import PartitionSpec as P


COEFFS = (0.75, -0.15, 1.0 / 60.0)
GAMMA_LESS = 0.4
HIGHEST = lax.Precision.HIGHEST

INST = 9
VARS = 5
PLANES = 2
ROWS = 8
WIDTH = 128
RING = 16
PAIRS = INST * VARS
PIECE = 3
SLOTS = RING * PIECE
LANES = SLOTS * ROWS
SENT = 40
GRANT = 16 * 2**20


def spectral_weights():
    return [0.5 * (-1.0) ** k / math.sin(math.pi * k / INST) for k in range(1, INST // 2 + 1)]


def tables():
    extent = WIDTH * RING
    eps = float(extent * extent // 16)
    rho = 2.0 * eps / (1.0 + 2.0 * eps + math.sqrt(1.0 + 4.0 * eps))
    gain = rho / (eps * (1.0 - rho * rho))
    lam = rho**WIDTH
    closing = 1.0 / (1.0 - lam**RING)
    at = np.arange(WIDTH)
    reach = np.zeros((WIDTH, WIDTH + 6))
    for k, weight in enumerate(COEFFS, 1):
        reach[at, at - k + 3] += weight
        reach[at, at + k + 3] -= weight
    spots = np.arange(-3, WIDTH + 3)
    green = gain * rho ** np.abs(at[:, None] - at[None, :])
    wide = gain * rho ** np.abs(spots[:, None] - at[None, :])
    local = np.concatenate([reach[:, 3:-3], reach @ wide, green], axis=1)
    rise = rho ** (WIDTH - 1.0 - at)
    fall = rho ** (at + 0.0)
    kappa = sum(weight * (rho**k - rho**-k) for k, weight in enumerate(COEFFS, 1))
    pick = np.zeros((16, WIDTH))
    pick[0:3, 0:3] = np.eye(3)
    pick[3:6, WIDTH - 3 :] = np.eye(3)
    pick[6] = kappa * rise
    pick[7] = -kappa * fall
    pick[8 + 6] = rise
    pick[8 + 7] = fall
    side = np.zeros((24, 2 * WIDTH))
    for c in range(3):
        for m in range(3):
            if 1 <= 3 + m - c <= 3:
                w = -COEFFS[3 + m - c - 1]
                side[3 + c, m] += w
                side[3 + c, WIDTH:] += w * gain * (rho ** np.abs(at - m) - rho ** (at - m + 0.0))
            if c + 1 + m <= 3:
                w = COEFFS[c + m]
                spot = WIDTH - 1 - m
                side[8 + c, spot] += w
                side[8 + c, WIDTH:] += w * gain * (
                    rho ** np.abs(at - spot) - rho ** (spot - at + 0.0)
                )
    side[16, WIDTH:] = gain * rho ** (at + 1.0)
    side[17, WIDTH:] = gain * rho ** (WIDTH - at + 0.0)
    sums = np.zeros((WIDTH, WIDTH))
    sums[:, 0:RING] = rise[:, None]
    sums[:, RING : 2 * RING] = fall[:, None]
    ring = np.arange(RING)
    powers = np.zeros((RING, WIDTH))
    powers[:, 0:RING] = closing * lam ** ((ring[None, :] - ring[:, None] - 1) % RING)
    powers[:, RING : 2 * RING] = closing * lam ** ((ring[:, None] - ring[None, :] - 1) % RING)
    return [np.asarray(t, np.float32) for t in (local, pick, side, sums, powers)]


def field(density, moments, v, a):
    return density[:, a] if v == 0 else moments[:, v - 1, a]


def dot(a, b, contract):
    return lax.dot_general(
        a, b, (contract, ((), ())), precision=HIGHEST, preferred_element_type=jnp.float32
    )


def row_index(shape):
    return lax.broadcasted_iota(jnp.int32, shape, len(shape) - 2)


def edge_kernel(density, moments, facing, sems):
    plane = 1 - lax.axis_index("axial")
    copies = []
    for v in range(VARS):
        source = density.at[:, plane] if v == 0 else moments.at[:, v - 1, plane]
        copies.append(
            pltpu.make_async_copy(source, facing.at[pl.ds(v * INST, INST)], sems.at[v])
        )
    for copy in copies:
        copy.start()
    facing[PAIRS:SLOTS] = jnp.zeros((SLOTS - PAIRS, ROWS, WIDTH), jnp.float32)
    for copy in copies:
        copy.wait()


def pack_kernel(density, moments, pick, first, last, cols, flux):
    low = row_index((INST, ROWS, WIDTH)) < 4
    for v in range(VARS):
        one, two = field(density, moments, v, 0), field(density, moments, v, 1)
        at = slice(v * INST, (v + 1) * INST)
        first[at] = jnp.where(low, one, pltpu.roll(two, 4, 1))
        last[at] = jnp.where(low, pltpu.roll(one, 4, 1), two)
    for a in range(PLANES):
        along = fluxes(*[field(density, moments, v, a) for v in range(VARS)], 2)
        put(flux, a, along)
    cols[...] = dot(pick[0:8], flux[...], ((1,), (1,)))


def put(ref, a, values):
    for v in range(VARS):
        at = (a * SLOTS + v * INST) * ROWS
        ref[at : at + INST * ROWS] = values[v].reshape(INST * ROWS, WIDTH)
    at = (a * SLOTS + PAIRS) * ROWS
    ref[at : (a + 1) * LANES] = jnp.zeros(((SLOTS - PAIRS) * ROWS, WIDTH), jnp.float32)


def fluxes(d, ma, mr, mp, e, dim):
    inverse = 1.0 / d
    pressure = GAMMA_LESS * (e - 0.5 * (ma * ma + mr * mr + mp * mp) * inverse)
    total = e + pressure
    if dim == 1:
        speed = mr * inverse
        return (mr, ma * speed, mr * speed + pressure, mp * speed, total * speed)
    speed = mp * inverse
    return (mp, ma * speed, mr * speed, mp * speed + pressure, total * speed)


def main_kernel(density, moments, above, below, local, pick, res, upd, sums, flux, rest):
    axial = lax.axis_index("axial")
    radial = lax.axis_index("radial")
    shape = (INST, ROWS, WIDTH)
    row = row_index(shape)
    low = row < 4
    known = jnp.where(low, (radial < lax.axis_size("radial") - 1).astype(jnp.int32), (radial > 0).astype(jnp.int32)) > 0
    weights = spectral_weights()
    for a in range(PLANES):
        fields = [field(density, moments, v, a) for v in range(VARS)]
        rims = []
        for v in range(VARS):
            at = slice(v * INST, (v + 1) * INST)
            up, down = above[at], below[at]
            if a == 0:
                rims.append(jnp.where(low, up, pltpu.roll(down, 4, 1)))
            else:
                rims.append(jnp.where(low, pltpu.roll(up, 4, 1), down))
        along_radial, beyond = fluxes(*fields, 1), fluxes(*rims, 1)
        put(flux, a, fluxes(*fields, 2))
        added = []
        mask = jnp.where(axial == 0, a == PLANES - 1, a == 0).astype(jnp.float32)
        for v in range(VARS):
            own, rim = along_radial[v], jnp.where(known, beyond[v], 0.0)
            total = -mask * fields[v]
            for k, weight in enumerate(COEFFS, 1):
                ahead = pltpu.roll(jnp.where(row >= k, own, rim), ROWS - k, 1)
                behind = pltpu.roll(jnp.where(row < ROWS - k, own, rim), k, 1)
                total = total + weight * (ahead - behind)
            f = fields[v]
            for k, weight in enumerate(weights, 1):
                back = jnp.concatenate([f[INST - k :], f[: INST - k]], axis=0)
                forth = jnp.concatenate([f[k:], f[:k]], axis=0)
                total = total + weight * (back - forth)
            added.append(total)
        put(rest, a, added)
    through = dot(flux[...], local[:, 0 : 2 * WIDTH], ((1,), (0,)))
    res[...] = rest[...] + through[:, 0:WIDTH]
    upd[...] = through[:, WIDTH:] + dot(rest[...], local[:, 2 * WIDTH :], ((1,), (0,)))
    sums[...] = dot(pick[0:8], flux[...], ((1,), (1,))) + dot(
        pick[8:16], rest[...], ((1,), (1,))
    )


def align_kernel(shifts, whole, sums, weigh, powers, out, rolled, kept):
    axial = lax.axis_index("axial")
    place = lax.axis_index("pitch")
    extent = WIDTH * RING
    tall = PIECE * ROWS
    lane = lax.broadcasted_iota(jnp.int32, (ROWS, WIDTH), 1)
    for j in range(PIECE):
        inst = lax.rem(place * PIECE + j, INST)
        shift = shifts[inst]
        offset = jnp.where(axial == 1, shift, (extent - shift) & (extent - 1))
        blocks, within = offset >> 7, offset & (WIDTH - 1)
        turned = pltpu.roll(whole[:, j], within, 2)
        rolled[0:RING] = turned
        rolled[RING : 2 * RING] = turned
        for d in range(RING):
            here = rolled[RING + d - blocks]
            before = rolled[RING - 1 + d - blocks]
            window = jnp.where(lane < within, before, here)
            at = d * SENT + j * ROWS
            out[at : at + ROWS] = window
            at = d * tall + j * ROWS
            kept[at : at + ROWS] = window
    totals = dot(kept[...], weigh[...], ((1,), (0,)))
    carried = totals[0:tall] * powers[0:1]
    for d in range(1, RING):
        carried = carried + totals[d * tall : (d + 1) * tall] * powers[d : d + 1]
    spread = powers[pl.ds(place, 1)]
    column = lax.broadcasted_iota(jnp.int32, (8, WIDTH), 1)
    line = row_index((8, WIDTH))
    extra = jnp.where(
        line == 0,
        jnp.where(column < RING, spread, 0.0),
        jnp.where((line == 1) & (column >= RING), spread, 0.0),
    )
    left = jnp.concatenate([carried, extra], axis=0)
    target = (1 - axial) * LANES + place * tall
    spots = lax.broadcasted_iota(jnp.int32, (tall, 2 * LANES), 1)
    select = (spots == target + row_index((tall, 2 * LANES))).astype(jnp.float32)
    right = jnp.concatenate([select, pltpu.roll(sums[...], 2, 0)], axis=0)
    carries = dot(left, right, ((0,), (0,)))
    for t in range(6):
        at = slice(t * WIDTH, (t + 1) * WIDTH)
        out[pl.ds(tall + t, RING, SENT)] = carries[0:RING, at]
        out[pl.ds(tall + 6 + t, RING, SENT)] = carries[RING : 2 * RING, at]


def final_kernel(res, upd, got, left, right, local, side, residual, update, first, second, sems):
    axial = lax.axis_index("axial")
    tall = PIECE * ROWS
    windows = got[:, 0:tall].reshape(LANES, WIDTH)
    smoothed = dot(windows, local[:, 2 * WIDTH :], ((1,), (0,)))
    carries = jnp.sum(got[:, tall:SENT], axis=0)
    line = row_index((8, WIDTH))
    copies = []
    for t in range(6):
        a, part = t // 3, t % 3
        at = slice(t * WIDTH, (t + 1) * WIDTH)
        pair = jnp.where(
            line == 0, carries[t : t + 1], jnp.where(line == 1, carries[6 + t : 7 + t], 0.0)
        )
        sides = jnp.concatenate([left[:, at], right[:, at], pair], axis=0)
        added = dot(sides, side[...], ((0,), (0,)))
        mine = axial == 1 - a
        here = slice(part * WIDTH, (part + 1) * WIDTH)
        r = res[at] + added[:, 0:WIDTH] + jnp.where(mine, windows[here], 0.0)
        u = upd[at] + added[:, WIDTH:] + jnp.where(mine, smoothed[here], 0.0)
        for j in range(16):
            pair_at = part * 16 + j
            if pair_at < PAIRS:
                v, n = pair_at // INST, pair_at % INST
                first[a, n, v] = r[j * ROWS : (j + 1) * ROWS]
                second[a, n, v] = u[j * ROWS : (j + 1) * ROWS]
        if part == 2:
            for i, (held, out) in enumerate(((first, residual), (second, update))):
                copy = pltpu.make_async_copy(held.at[a], out.at[:, :, a], sems.at[2 * a + i])
                copy.start()
                copies.append(copy)
    for copy in copies:
        copy.wait()


def call(kernel, outs, scratch=(), scalars=0, work=(0, 0), inputs=0):
    vmem = pl.BlockSpec(memory_space=pltpu.VMEM)
    smem = pl.BlockSpec(memory_space=pltpu.SMEM)
    return pl.pallas_call(
        kernel,
        out_shape=[jax.ShapeDtypeStruct(s, jnp.float32) for s in outs],
        in_specs=[smem] * scalars + [vmem] * inputs,
        out_specs=[vmem] * len(outs),
        scratch_shapes=[pltpu.VMEM(s, jnp.float32) for s in scratch],
        cost_estimate=pl.CostEstimate(flops=work[0], bytes_accessed=work[1], transcendentals=0),
        compiler_params=pltpu.CompilerParams(vmem_limit_bytes=GRANT),
    )


def local_step(density, moments, shifts):
    local, pick, side, weigh, powers = [jnp.asarray(t) for t in tables()]
    height = PLANES * LANES
    facing = pl.pallas_call(
        edge_kernel,
        out_shape=jax.ShapeDtypeStruct((SLOTS, ROWS, WIDTH), jnp.float32),
        in_specs=[pl.BlockSpec(memory_space=pl.ANY)] * 2,
        out_specs=pl.BlockSpec(memory_space=pltpu.VMEM),
        scratch_shapes=[pltpu.SemaphoreType.DMA((VARS,))],
    )(density, moments)
    across = lax.ppermute(facing, "axial", [(0, 1), (1, 0)])
    first, last, cols = call(
        pack_kernel,
        [(PAIRS, ROWS, WIDTH), (PAIRS, ROWS, WIDTH), (8, height)],
        scratch=[(height, WIDTH)],
        inputs=3,
        work=(10**6, 10**6),
    )(density, moments, pick)
    count_r = lax.axis_size("radial")
    up = [(i, i + 1) for i in range(count_r - 1)]
    down = [(j, i) for i, j in up]
    above = lax.ppermute(first, "radial", down)
    below = lax.ppermute(last, "radial", up)
    ring = [(i, (i + 1) % RING) for i in range(RING)]
    back = [(j, i) for i, j in ring]
    left = lax.ppermute(cols, "pitch", ring)
    right = lax.ppermute(cols, "pitch", back)
    whole = lax.all_to_all(across.reshape(RING, PIECE, ROWS, WIDTH), "pitch", 0, 0)
    res, upd, sums = call(
        main_kernel,
        [(height, WIDTH), (height, WIDTH), (8, height)],
        scratch=[(height, WIDTH), (height, WIDTH)],
        inputs=6,
        work=(10**8, 2 * 10**6),
    )(density, moments, above, below, local, pick)
    (send,) = call(
        align_kernel,
        [(RING * SENT, WIDTH)],
        scratch=[(2 * RING, ROWS, WIDTH), (RING * PIECE * ROWS, WIDTH)],
        scalars=1,
        inputs=4,
        work=(10**7, 10**6),
    )(shifts, whole, sums, weigh, powers)
    send, left, right = lax.optimization_barrier((send, left, right))
    got = lax.all_to_all(send.reshape(RING, SENT, WIDTH), "pitch", 0, 0)
    shape = (INST, VARS, PLANES, ROWS, WIDTH)
    held = pltpu.VMEM((PLANES, INST, VARS, ROWS, WIDTH), jnp.float32)
    return pl.pallas_call(
        final_kernel,
        out_shape=[jax.ShapeDtypeStruct(shape, jnp.float32)] * 2,
        in_specs=[pl.BlockSpec(memory_space=pltpu.VMEM)] * 7,
        out_specs=[pl.BlockSpec(memory_space=pl.ANY)] * 2,
        scratch_shapes=[held, held, pltpu.SemaphoreType.DMA((2 * PLANES,))],
        cost_estimate=pl.CostEstimate(flops=10**7, bytes_accessed=2 * 10**6, transcendentals=0),
        compiler_params=pltpu.CompilerParams(vmem_limit_bytes=GRANT),
    )(res, upd, got, left, right, local, side)


def solution(mesh):
    in_specs = (P(None, "axial", "radial", "pitch"), P(None, None, "axial", "radial", "pitch"), P())
    out_specs = (
        P(None, None, "axial", "radial", "pitch"),
        P(None, None, "axial", "radial", "pitch"),
    )
    return jax.shard_map(
        local_step, mesh=mesh, in_specs=in_specs, out_specs=out_specs, check_vma=False
    )
```

```python
import math

import jax
import jax.numpy as jnp
import numpy as np
from jax import lax
from jax.experimental import pallas as pl
from jax.experimental.pallas import tpu as pltpu
from jax.sharding import PartitionSpec as P


COEFFS = (0.75, -0.15, 1.0 / 60.0)
GAMMA_LESS = 0.4
HIGHEST = lax.Precision.HIGHEST

INST = 9
VARS = 5
PLANES = 2
ROWS = 8
WIDTH = 128
RING = 16
PAIRS = INST * VARS
PIECE = 3
SLOTS = RING * PIECE
LANES = SLOTS * ROWS
SENT = 36
GRANT = 16 * 2**20


def spectral_weights():
    return [0.5 * (-1.0) ** k / math.sin(math.pi * k / INST) for k in range(1, INST // 2 + 1)]


def tables():
    extent = WIDTH * RING
    eps = float(extent * extent // 16)
    rho = 2.0 * eps / (1.0 + 2.0 * eps + math.sqrt(1.0 + 4.0 * eps))
    gain = rho / (eps * (1.0 - rho * rho))
    lam = rho**WIDTH
    closing = 1.0 / (1.0 - lam**RING)
    at = np.arange(WIDTH)
    reach = np.zeros((WIDTH, WIDTH + 6))
    for k, weight in enumerate(COEFFS, 1):
        reach[at, at - k + 3] += weight
        reach[at, at + k + 3] -= weight
    spots = np.arange(-3, WIDTH + 3)
    green = gain * rho ** np.abs(at[:, None] - at[None, :])
    wide = gain * rho ** np.abs(spots[:, None] - at[None, :])
    local = np.concatenate([reach[:, 3:-3], reach @ wide, green], axis=1)
    rise = rho ** (WIDTH - 1.0 - at)
    fall = rho ** (at + 0.0)
    kappa = sum(weight * (rho**k - rho**-k) for k, weight in enumerate(COEFFS, 1))
    pick = np.zeros((16, WIDTH))
    pick[0:3, 0:3] = np.eye(3)
    pick[3:6, WIDTH - 3 :] = np.eye(3)
    pick[6] = kappa * rise
    pick[7] = -kappa * fall
    pick[8 + 6] = rise
    pick[8 + 7] = fall
    side = np.zeros((24, 2 * WIDTH))
    for c in range(3):
        for m in range(3):
            if 1 <= 3 + m - c <= 3:
                w = -COEFFS[3 + m - c - 1]
                side[3 + c, m] += w
                side[3 + c, WIDTH:] += w * gain * (rho ** np.abs(at - m) - rho ** (at - m + 0.0))
            if c + 1 + m <= 3:
                w = COEFFS[c + m]
                spot = WIDTH - 1 - m
                side[8 + c, spot] += w
                side[8 + c, WIDTH:] += w * gain * (
                    rho ** np.abs(at - spot) - rho ** (spot - at + 0.0)
                )
    side[16, WIDTH:] = gain * rho ** (at + 1.0)
    side[17, WIDTH:] = gain * rho ** (WIDTH - at + 0.0)
    sums = np.zeros((WIDTH, WIDTH))
    sums[:, 0:RING] = rise[:, None]
    sums[:, RING : 2 * RING] = fall[:, None]
    ring = np.arange(RING)
    powers = np.zeros((RING, WIDTH))
    powers[:, 0:RING] = closing * lam ** ((ring[None, :] - ring[:, None] - 1) % RING)
    powers[:, RING : 2 * RING] = closing * lam ** ((ring[:, None] - ring[None, :] - 1) % RING)
    return [np.asarray(t, np.float32) for t in (local, pick, side, sums, powers)]


def field(density, moments, v, a):
    return density[:, a] if v == 0 else moments[:, v - 1, a]


def dot(a, b, contract):
    return lax.dot_general(
        a, b, (contract, ((), ())), precision=HIGHEST, preferred_element_type=jnp.float32
    )


def split(a):
    high = a.astype(jnp.bfloat16)
    return high, (a - high.astype(jnp.float32)).astype(jnp.bfloat16)


def dot3(a, b, contract):
    (ah, al), (bh, bl) = split(a), split(b)

    def one(x, y):
        return lax.dot_general(x, y, (contract, ((), ())), preferred_element_type=jnp.float32)

    return one(ah, bh) + (one(ah, bl) + one(al, bh))


def row_index(shape):
    return lax.broadcasted_iota(jnp.int32, shape, len(shape) - 2)


def edge_kernel(density, moments, facing, held, sems):
    plane = 1 - lax.axis_index("axial")
    reads, writes = [], []
    for v in range(VARS):
        source = density.at[:, plane] if v == 0 else moments.at[:, v - 1, plane]
        at = pl.ds(v * INST, INST)
        reads.append(pltpu.make_async_copy(source, held.at[at], sems.at[v]))
        writes.append(pltpu.make_async_copy(held.at[at], facing.at[at], sems.at[VARS + v]))
    at = pl.ds(PAIRS, SLOTS - PAIRS)
    for read in reads:
        read.start()
    held[PAIRS:SLOTS] = jnp.zeros((SLOTS - PAIRS, ROWS, WIDTH), jnp.float32)
    writes.append(pltpu.make_async_copy(held.at[at], facing.at[at], sems.at[2 * VARS]))
    for read, write in zip(reads, writes):
        read.wait()
        write.start()
    writes[-1].start()
    for write in writes:
        write.wait()


def pack_kernel(shifts, density, moments, pick, inside, outside, cols, turns, flux):
    axial, place = lax.axis_index("axial"), lax.axis_index("pitch")
    extent = WIDTH * RING
    for j in range(PIECE):
        shift = shifts[lax.rem(place * PIECE + j, INST)]
        turns[j] = jnp.where(axial == 1, shift, (extent - shift) & (extent - 1))
    even = lax.rem(lax.axis_index("radial"), 2) == 0
    low = row_index((INST, ROWS, WIDTH)) < 4
    for v in range(VARS):
        one, two = field(density, moments, v, 0), field(density, moments, v, 1)
        at = slice(v * INST, (v + 1) * INST)
        first = jnp.where(low, one, pltpu.roll(two, 4, 1))
        last = jnp.where(low, pltpu.roll(one, 4, 1), two)
        inside[at] = jnp.where(even, last, first)
        outside[at] = jnp.where(even, first, last)
    for a in range(PLANES):
        along = fluxes(*[field(density, moments, v, a) for v in range(VARS)], 2)
        put(flux, a, along)
    cols[...] = dot(pick[0:8], flux[...], ((1,), (1,)))


def put(ref, a, values):
    for v in range(VARS):
        at = (a * SLOTS + v * INST) * ROWS
        ref[at : at + INST * ROWS] = values[v].reshape(INST * ROWS, WIDTH)
    at = (a * SLOTS + PAIRS) * ROWS
    ref[at : (a + 1) * LANES] = jnp.zeros(((SLOTS - PAIRS) * ROWS, WIDTH), jnp.float32)


def fluxes(d, ma, mr, mp, e, dim):
    inverse = 1.0 / d
    pressure = GAMMA_LESS * (e - 0.5 * (ma * ma + mr * mr + mp * mp) * inverse)
    total = e + pressure
    if dim == 1:
        speed = mr * inverse
        return (mr, ma * speed, mr * speed + pressure, mp * speed, total * speed)
    speed = mp * inverse
    return (mp, ma * speed, mr * speed, mp * speed + pressure, total * speed)


def main_kernel(density, moments, inside, outside, local, pick, res, upd, sums, flux, rest):
    axial = lax.axis_index("axial")
    radial = lax.axis_index("radial")
    even = lax.rem(radial, 2) == 0
    shape = (INST, ROWS, WIDTH)
    row = row_index(shape)
    low = row < 4
    known = jnp.where(low, (radial < lax.axis_size("radial") - 1).astype(jnp.int32), (radial > 0).astype(jnp.int32)) > 0
    weights = spectral_weights()
    for a in range(PLANES):
        fields = [field(density, moments, v, a) for v in range(VARS)]
        rims = []
        for v in range(VARS):
            at = slice(v * INST, (v + 1) * INST)
            near, far = inside[at], outside[at]
            up, down = jnp.where(even, near, far), jnp.where(even, far, near)
            if a == 0:
                rims.append(jnp.where(low, up, pltpu.roll(down, 4, 1)))
            else:
                rims.append(jnp.where(low, pltpu.roll(up, 4, 1), down))
        along_radial, beyond = fluxes(*fields, 1), fluxes(*rims, 1)
        put(flux, a, fluxes(*fields, 2))
        added = []
        mask = jnp.where(axial == 0, a == PLANES - 1, a == 0).astype(jnp.float32)
        for v in range(VARS):
            own, rim = along_radial[v], jnp.where(known, beyond[v], 0.0)
            total = -mask * fields[v]
            for k, weight in enumerate(COEFFS, 1):
                ahead = pltpu.roll(jnp.where(row >= k, own, rim), ROWS - k, 1)
                behind = pltpu.roll(jnp.where(row < ROWS - k, own, rim), k, 1)
                total = total + weight * (ahead - behind)
            f = fields[v]
            for k, weight in enumerate(weights, 1):
                back = jnp.concatenate([f[INST - k :], f[: INST - k]], axis=0)
                forth = jnp.concatenate([f[k:], f[:k]], axis=0)
                total = total + weight * (back - forth)
            added.append(total)
        put(rest, a, added)
    through = dot(flux[...], local[:, 0 : 2 * WIDTH], ((1,), (0,)))
    res[...] = rest[...] + through[:, 0:WIDTH]
    upd[...] = through[:, WIDTH:] + dot(rest[...], local[:, 2 * WIDTH :], ((1,), (0,)))
    sums[...] = dot(pick[0:8], flux[...], ((1,), (1,))) + dot(
        pick[8:16], rest[...], ((1,), (1,))
    )


def align_kernel(turns, whole, sums, weigh, powers, out, rolled, kept):
    axial = lax.axis_index("axial")
    place = lax.axis_index("pitch")
    tall = PIECE * ROWS
    lane = lax.broadcasted_iota(jnp.int32, (ROWS, WIDTH), 1)
    for j in range(PIECE):
        blocks, within = turns[j] >> 7, turns[j] & (WIDTH - 1)
        turned = pltpu.roll(whole[:, j], within, 2)
        rolled[0:RING] = turned
        rolled[RING : 2 * RING] = turned
        for d in range(RING):
            here = rolled[RING + d - blocks]
            before = rolled[RING - 1 + d - blocks]
            window = jnp.where(lane < within, before, here)
            at = d * SENT + j * ROWS
            out[at : at + ROWS] = window
            at = d * tall + j * ROWS
            kept[at : at + ROWS] = window
    totals = dot3(kept[...], weigh[...], ((1,), (0,)))
    carried = totals[0:tall] * powers[0:1]
    for d in range(1, RING):
        carried = carried + totals[d * tall : (d + 1) * tall] * powers[d : d + 1]
    spread = powers[pl.ds(place, 1)]
    column = lax.broadcasted_iota(jnp.int32, (8, WIDTH), 1)
    line = row_index((8, WIDTH))
    extra = jnp.where(
        line == 0,
        jnp.where(column < RING, spread, 0.0),
        jnp.where((line == 1) & (column >= RING), spread, 0.0),
    )
    left = jnp.concatenate([carried, extra], axis=0)
    target = (1 - axial) * LANES + place * tall
    spots = lax.broadcasted_iota(jnp.int32, (tall, 2 * LANES), 1)
    select = (spots == target + row_index((tall, 2 * LANES))).astype(jnp.float32)
    right = jnp.concatenate([select, pltpu.roll(sums[...], 2, 0)], axis=0)
    carries = dot3(left[:, 0 : 2 * RING], right, ((0,), (0,)))
    for t in range(6):
        at = slice(t * WIDTH, (t + 1) * WIDTH)
        out[pl.ds(tall + t, RING, SENT)] = carries[0:RING, at]
        out[pl.ds(tall + 6 + t, RING, SENT)] = carries[RING : 2 * RING, at]


def final_kernel(res, upd, got, left, right, local, side, residual, update, first, second, sems):
    axial = lax.axis_index("axial")
    tall = PIECE * ROWS
    windows = jnp.concatenate([got[h * SENT : h * SENT + tall] for h in range(RING)], axis=0)
    smoothed = dot3(windows, local[:, 2 * WIDTH :], ((1,), (0,)))
    carries = got[tall:SENT]
    for h in range(1, RING):
        carries = carries + got[h * SENT + tall : (h + 1) * SENT]
    line = row_index((8, WIDTH))
    copies = []
    for t in range(6):
        a, part = t // 3, t % 3
        at = slice(t * WIDTH, (t + 1) * WIDTH)
        pair = jnp.where(
            line == 0, carries[t : t + 1], jnp.where(line == 1, carries[6 + t : 7 + t], 0.0)
        )
        sides = jnp.concatenate([left[:, at], right[:, at], pair], axis=0)
        added = dot3(sides, side[...], ((0,), (0,)))
        mine = axial == 1 - a
        here = slice(part * WIDTH, (part + 1) * WIDTH)
        r = res[at] + added[:, 0:WIDTH] + jnp.where(mine, windows[here], 0.0)
        u = upd[at] + added[:, WIDTH:] + jnp.where(mine, smoothed[here], 0.0)
        for j in range(16):
            pair_at = part * 16 + j
            if pair_at < PAIRS:
                v, n = pair_at // INST, pair_at % INST
                first[a, n, v] = r[j * ROWS : (j + 1) * ROWS]
                second[a, n, v] = u[j * ROWS : (j + 1) * ROWS]
        if part == 2:
            for i, (held, out) in enumerate(((first, residual), (second, update))):
                copy = pltpu.make_async_copy(held.at[a], out.at[:, :, a], sems.at[2 * a + i])
                copy.start()
                copies.append(copy)
    for copy in copies:
        copy.wait()


def call(kernel, outs, scratch=(), scalars=0, work=(0, 0), inputs=0):
    vmem = pl.BlockSpec(memory_space=pltpu.VMEM)
    smem = pl.BlockSpec(memory_space=pltpu.SMEM)
    return pl.pallas_call(
        kernel,
        out_shape=[jax.ShapeDtypeStruct(s, jnp.float32) for s in outs],
        in_specs=[smem] * scalars + [vmem] * inputs,
        out_specs=[vmem] * len(outs),
        scratch_shapes=[pltpu.VMEM(s, jnp.float32) for s in scratch],
        cost_estimate=pl.CostEstimate(flops=work[0], bytes_accessed=work[1], transcendentals=0),
        compiler_params=pltpu.CompilerParams(vmem_limit_bytes=GRANT),
    )


def local_step(density, moments, shifts):
    local, pick, side, weigh, powers = [jnp.asarray(t) for t in tables()]
    height = PLANES * LANES
    facing = pl.pallas_call(
        edge_kernel,
        out_shape=jax.ShapeDtypeStruct((SLOTS, ROWS, WIDTH), jnp.float32),
        in_specs=[pl.BlockSpec(memory_space=pl.ANY)] * 2,
        out_specs=pl.BlockSpec(memory_space=pl.ANY),
        scratch_shapes=[
            pltpu.VMEM((SLOTS, ROWS, WIDTH), jnp.float32),
            pltpu.SemaphoreType.DMA((2 * VARS + 1,)),
        ],
    )(density, moments)
    across = lax.ppermute(facing, "axial", [(0, 1), (1, 0)])
    vmem = pl.BlockSpec(memory_space=pltpu.VMEM)
    smem = pl.BlockSpec(memory_space=pltpu.SMEM)
    halo = jax.ShapeDtypeStruct((PAIRS, ROWS, WIDTH), jnp.float32)
    inside, outside, cols, turns = pl.pallas_call(
        pack_kernel,
        out_shape=[
            halo,
            halo,
            jax.ShapeDtypeStruct((8, height), jnp.float32),
            jax.ShapeDtypeStruct((PIECE,), jnp.int32),
        ],
        in_specs=[smem, vmem, vmem, vmem],
        out_specs=[vmem, vmem, vmem, smem],
        scratch_shapes=[pltpu.VMEM((height, WIDTH), jnp.float32)],
        cost_estimate=pl.CostEstimate(flops=10**6, bytes_accessed=10**6, transcendentals=0),
        compiler_params=pltpu.CompilerParams(vmem_limit_bytes=GRANT),
    )(shifts, density, moments, pick)
    count_r = lax.axis_size("radial")
    pairs = [(i, i ^ 1) for i in range(count_r)]
    between = [(i, i - 1 if i % 2 == 0 else i + 1) for i in range(1, count_r - 1)]
    inside = lax.ppermute(inside, "radial", pairs)
    outside = lax.ppermute(outside, "radial", between)
    ring = [(i, (i + 1) % RING) for i in range(RING)]
    back = [(j, i) for i, j in ring]
    left = lax.ppermute(cols, "pitch", ring)
    right = lax.ppermute(cols, "pitch", back)
    whole = lax.all_to_all(across.reshape(RING, PIECE, ROWS, WIDTH), "pitch", 0, 0)
    res, upd, sums = call(
        main_kernel,
        [(height, WIDTH), (height, WIDTH), (8, height)],
        scratch=[(height, WIDTH), (height, WIDTH)],
        inputs=6,
        work=(10**8, 2 * 10**6),
    )(density, moments, inside, outside, local, pick)
    (send,) = call(
        align_kernel,
        [(RING * SENT, WIDTH)],
        scratch=[(2 * RING, ROWS, WIDTH), (RING * PIECE * ROWS, WIDTH)],
        scalars=1,
        inputs=4,
        work=(10**7, 10**6),
    )(turns, whole, sums, weigh, powers)
    send, left, right = lax.optimization_barrier((send, left, right))
    got = lax.all_to_all(send.reshape(RING, SENT // 4, 4, WIDTH), "pitch", 0, 0)
    got = got.reshape(RING * SENT, WIDTH)
    shape = (INST, VARS, PLANES, ROWS, WIDTH)
    held = pltpu.VMEM((PLANES, INST, VARS, ROWS, WIDTH), jnp.float32)
    return pl.pallas_call(
        final_kernel,
        out_shape=[jax.ShapeDtypeStruct(shape, jnp.float32)] * 2,
        in_specs=[pl.BlockSpec(memory_space=pltpu.VMEM)] * 7,
        out_specs=[pl.BlockSpec(memory_space=pl.ANY)] * 2,
        scratch_shapes=[held, held, pltpu.SemaphoreType.DMA((2 * PLANES,))],
        cost_estimate=pl.CostEstimate(flops=10**7, bytes_accessed=2 * 10**6, transcendentals=0),
        compiler_params=pltpu.CompilerParams(vmem_limit_bytes=GRANT),
    )(res, upd, got, left, right, local, side)


def solution(mesh):
    in_specs = (P(None, "axial", "radial", "pitch"), P(None, None, "axial", "radial", "pitch"), P())
    out_specs = (
        P(None, None, "axial", "radial", "pitch"),
        P(None, None, "axial", "radial", "pitch"),
    )
    return jax.shard_map(
        local_step, mesh=mesh, in_specs=in_specs, out_specs=out_specs, check_vma=False
    )
```

```python
import math

import jax
import jax.numpy as jnp
import numpy as np
from jax import lax
from jax.experimental import pallas as pl
from jax.experimental.pallas import tpu as pltpu
from jax.sharding import PartitionSpec as P


COEFFS = (0.75, -0.15, 1.0 / 60.0)
GAMMA_LESS = 0.4
HIGHEST = lax.Precision.HIGHEST

INST = 9
VARS = 5
PLANES = 2
ROWS = 8
WIDTH = 128
RING = 16
PAIRS = INST * VARS
PIECE = 3
SLOTS = RING * PIECE
LANES = SLOTS * ROWS
SENT = 36
GRANT = 16 * 2**20


def spectral_weights():
    return [0.5 * (-1.0) ** k / math.sin(math.pi * k / INST) for k in range(1, INST // 2 + 1)]


def tables():
    extent = WIDTH * RING
    eps = float(extent * extent // 16)
    rho = 2.0 * eps / (1.0 + 2.0 * eps + math.sqrt(1.0 + 4.0 * eps))
    gain = rho / (eps * (1.0 - rho * rho))
    lam = rho**WIDTH
    closing = 1.0 / (1.0 - lam**RING)
    at = np.arange(WIDTH)
    reach = np.zeros((WIDTH, WIDTH + 6))
    for k, weight in enumerate(COEFFS, 1):
        reach[at, at - k + 3] += weight
        reach[at, at + k + 3] -= weight
    spots = np.arange(-3, WIDTH + 3)
    green = gain * rho ** np.abs(at[:, None] - at[None, :])
    wide = gain * rho ** np.abs(spots[:, None] - at[None, :])
    local = np.concatenate([reach[:, 3:-3], reach @ wide, green], axis=1)
    rise = rho ** (WIDTH - 1.0 - at)
    fall = rho ** (at + 0.0)
    kappa = sum(weight * (rho**k - rho**-k) for k, weight in enumerate(COEFFS, 1))
    pick = np.zeros((16, WIDTH))
    pick[0:3, 0:3] = np.eye(3)
    pick[3:6, WIDTH - 3 :] = np.eye(3)
    pick[6] = kappa * rise
    pick[7] = -kappa * fall
    pick[8 + 6] = rise
    pick[8 + 7] = fall
    side = np.zeros((24, 2 * WIDTH))
    for c in range(3):
        for m in range(3):
            if 1 <= 3 + m - c <= 3:
                w = -COEFFS[3 + m - c - 1]
                side[3 + c, m] += w
                side[3 + c, WIDTH:] += w * gain * (rho ** np.abs(at - m) - rho ** (at - m + 0.0))
            if c + 1 + m <= 3:
                w = COEFFS[c + m]
                spot = WIDTH - 1 - m
                side[8 + c, spot] += w
                side[8 + c, WIDTH:] += w * gain * (
                    rho ** np.abs(at - spot) - rho ** (spot - at + 0.0)
                )
    side[16, WIDTH:] = gain * rho ** (at + 1.0)
    side[17, WIDTH:] = gain * rho ** (WIDTH - at + 0.0)
    sums = np.zeros((WIDTH, WIDTH))
    sums[:, 0:RING] = rise[:, None]
    sums[:, RING : 2 * RING] = fall[:, None]
    ring = np.arange(RING)
    powers = np.zeros((RING, WIDTH))
    powers[:, 0:RING] = closing * lam ** ((ring[None, :] - ring[:, None] - 1) % RING)
    powers[:, RING : 2 * RING] = closing * lam ** ((ring[:, None] - ring[None, :] - 1) % RING)
    return [np.asarray(t, np.float32) for t in (local, pick, side, sums, powers)]


def field(density, moments, v, a):
    return density[:, a] if v == 0 else moments[:, v - 1, a]


def dot(a, b, contract):
    return lax.dot_general(
        a, b, (contract, ((), ())), precision=HIGHEST, preferred_element_type=jnp.float32
    )


def split(a):
    high = a.astype(jnp.bfloat16)
    return high, (a - high.astype(jnp.float32)).astype(jnp.bfloat16)


def dot3(a, b, contract):
    (ah, al), (bh, bl) = split(a), split(b)

    def one(x, y):
        return lax.dot_general(x, y, (contract, ((), ())), preferred_element_type=jnp.float32)

    return one(ah, bh) + (one(ah, bl) + one(al, bh))


def row_index(shape):
    return lax.broadcasted_iota(jnp.int32, shape, len(shape) - 2)


def edge_kernel(density, moments, facing, sems):
    plane = 1 - lax.axis_index("axial")
    copies = []
    for v in range(VARS):
        source = density.at[:, plane] if v == 0 else moments.at[:, v - 1, plane]
        copies.append(
            pltpu.make_async_copy(source, facing.at[pl.ds(v * INST, INST)], sems.at[v])
        )
    for copy in copies:
        copy.start()
    facing[PAIRS:SLOTS] = jnp.zeros((SLOTS - PAIRS, ROWS, WIDTH), jnp.float32)
    for copy in copies:
        copy.wait()


def pack_kernel(shifts, density, moments, pick, inside, outside, cols, turns, flux):
    axial, place = lax.axis_index("axial"), lax.axis_index("pitch")
    extent = WIDTH * RING
    for j in range(PIECE):
        shift = shifts[lax.rem(place * PIECE + j, INST)]
        turns[j] = jnp.where(axial == 1, shift, (extent - shift) & (extent - 1))
    even = lax.rem(lax.axis_index("radial"), 2) == 0
    low = row_index((INST, ROWS, WIDTH)) < 4
    for v in range(VARS):
        one, two = field(density, moments, v, 0), field(density, moments, v, 1)
        at = slice(v * INST, (v + 1) * INST)
        first = jnp.where(low, one, pltpu.roll(two, 4, 1))
        last = jnp.where(low, pltpu.roll(one, 4, 1), two)
        inside[at] = jnp.where(even, last, first)
        outside[at] = jnp.where(even, first, last)
    for a in range(PLANES):
        along = fluxes(*[field(density, moments, v, a) for v in range(VARS)], 2)
        put(flux, a, along)
    cols[...] = dot(pick[0:8], flux[...], ((1,), (1,)))


def put(ref, a, values):
    for v in range(VARS):
        at = (a * SLOTS + v * INST) * ROWS
        ref[at : at + INST * ROWS] = values[v].reshape(INST * ROWS, WIDTH)
    at = (a * SLOTS + PAIRS) * ROWS
    ref[at : (a + 1) * LANES] = jnp.zeros(((SLOTS - PAIRS) * ROWS, WIDTH), jnp.float32)


def fluxes(d, ma, mr, mp, e, dim):
    inverse = 1.0 / d
    pressure = GAMMA_LESS * (e - 0.5 * (ma * ma + mr * mr + mp * mp) * inverse)
    total = e + pressure
    if dim == 1:
        speed = mr * inverse
        return (mr, ma * speed, mr * speed + pressure, mp * speed, total * speed)
    speed = mp * inverse
    return (mp, ma * speed, mr * speed, mp * speed + pressure, total * speed)


def main_kernel(density, moments, inside, outside, local, pick, res, upd, sums, flux, rest):
    axial = lax.axis_index("axial")
    radial = lax.axis_index("radial")
    even = lax.rem(radial, 2) == 0
    shape = (INST, ROWS, WIDTH)
    row = row_index(shape)
    low = row < 4
    known = jnp.where(low, (radial < lax.axis_size("radial") - 1).astype(jnp.int32), (radial > 0).astype(jnp.int32)) > 0
    weights = spectral_weights()
    for a in range(PLANES):
        fields = [field(density, moments, v, a) for v in range(VARS)]
        rims = []
        for v in range(VARS):
            at = slice(v * INST, (v + 1) * INST)
            near, far = inside[at], outside[at]
            up, down = jnp.where(even, near, far), jnp.where(even, far, near)
            if a == 0:
                rims.append(jnp.where(low, up, pltpu.roll(down, 4, 1)))
            else:
                rims.append(jnp.where(low, pltpu.roll(up, 4, 1), down))
        along_radial, beyond = fluxes(*fields, 1), fluxes(*rims, 1)
        put(flux, a, fluxes(*fields, 2))
        added = []
        mask = jnp.where(axial == 0, a == PLANES - 1, a == 0).astype(jnp.float32)
        for v in range(VARS):
            own, rim = along_radial[v], jnp.where(known, beyond[v], 0.0)
            total = -mask * fields[v]
            for k, weight in enumerate(COEFFS, 1):
                ahead = pltpu.roll(jnp.where(row >= k, own, rim), ROWS - k, 1)
                behind = pltpu.roll(jnp.where(row < ROWS - k, own, rim), k, 1)
                total = total + weight * (ahead - behind)
            f = fields[v]
            for k, weight in enumerate(weights, 1):
                back = jnp.concatenate([f[INST - k :], f[: INST - k]], axis=0)
                forth = jnp.concatenate([f[k:], f[:k]], axis=0)
                total = total + weight * (back - forth)
            added.append(total)
        put(rest, a, added)
    through = dot(flux[...], local[:, 0 : 2 * WIDTH], ((1,), (0,)))
    res[...] = rest[...] + through[:, 0:WIDTH]
    upd[...] = through[:, WIDTH:] + dot(rest[...], local[:, 2 * WIDTH :], ((1,), (0,)))
    sums[...] = dot(pick[0:8], flux[...], ((1,), (1,))) + dot(
        pick[8:16], rest[...], ((1,), (1,))
    )


def align_kernel(turns, whole, sums, weigh, powers, out, rolled, kept):
    axial = lax.axis_index("axial")
    place = lax.axis_index("pitch")
    tall = PIECE * ROWS
    lane = lax.broadcasted_iota(jnp.int32, (ROWS, WIDTH), 1)
    for j in range(PIECE):
        blocks, within = turns[j] >> 7, turns[j] & (WIDTH - 1)
        turned = pltpu.roll(whole[:, j], within, 2)
        rolled[0:RING] = turned
        rolled[RING : 2 * RING] = turned
        for d in range(RING):
            here = rolled[RING + d - blocks]
            before = rolled[RING - 1 + d - blocks]
            window = jnp.where(lane < within, before, here)
            at = d * SENT + j * ROWS
            out[at : at + ROWS] = window
            at = d * tall + j * ROWS
            kept[at : at + ROWS] = window
    totals = dot3(kept[...], weigh[...], ((1,), (0,)))
    carried = totals[0:tall] * powers[0:1]
    for d in range(1, RING):
        carried = carried + totals[d * tall : (d + 1) * tall] * powers[d : d + 1]
    spread = powers[pl.ds(place, 1)]
    column = lax.broadcasted_iota(jnp.int32, (8, WIDTH), 1)
    line = row_index((8, WIDTH))
    extra = jnp.where(
        line == 0,
        jnp.where(column < RING, spread, 0.0),
        jnp.where((line == 1) & (column >= RING), spread, 0.0),
    )
    left = jnp.concatenate([carried, extra], axis=0)
    target = (1 - axial) * LANES + place * tall
    spots = lax.broadcasted_iota(jnp.int32, (tall, 2 * LANES), 1)
    select = (spots == target + row_index((tall, 2 * LANES))).astype(jnp.float32)
    right = jnp.concatenate([select, pltpu.roll(sums[...], 2, 0)], axis=0)
    carries = dot3(left[:, 0 : 2 * RING], right, ((0,), (0,)))
    for t in range(6):
        at = slice(t * WIDTH, (t + 1) * WIDTH)
        out[pl.ds(tall + t, RING, SENT)] = carries[0:RING, at]
        out[pl.ds(tall + 6 + t, RING, SENT)] = carries[RING : 2 * RING, at]


def final_kernel(res, upd, got, left, right, local, side, residual, update, first, second, sems):
    axial = lax.axis_index("axial")
    tall = PIECE * ROWS
    windows = jnp.concatenate([got[h * SENT : h * SENT + tall] for h in range(RING)], axis=0)
    smoothed = dot3(windows, local[:, 2 * WIDTH :], ((1,), (0,)))
    carries = got[tall:SENT]
    for h in range(1, RING):
        carries = carries + got[h * SENT + tall : (h + 1) * SENT]
    line = row_index((8, WIDTH))
    copies = []
    for t in range(6):
        a, part = t // 3, t % 3
        at = slice(t * WIDTH, (t + 1) * WIDTH)
        pair = jnp.where(
            line == 0, carries[t : t + 1], jnp.where(line == 1, carries[6 + t : 7 + t], 0.0)
        )
        sides = jnp.concatenate([left[:, at], right[:, at], pair], axis=0)
        added = dot3(sides, side[...], ((0,), (0,)))
        mine = axial == 1 - a
        here = slice(part * WIDTH, (part + 1) * WIDTH)
        r = res[at] + added[:, 0:WIDTH] + jnp.where(mine, windows[here], 0.0)
        u = upd[at] + added[:, WIDTH:] + jnp.where(mine, smoothed[here], 0.0)
        for j in range(16):
            pair_at = part * 16 + j
            if pair_at < PAIRS:
                v, n = pair_at // INST, pair_at % INST
                first[a, n, v] = r[j * ROWS : (j + 1) * ROWS]
                second[a, n, v] = u[j * ROWS : (j + 1) * ROWS]
        if part == 2:
            for i, (held, out) in enumerate(((first, residual), (second, update))):
                copy = pltpu.make_async_copy(held.at[a], out.at[:, :, a], sems.at[2 * a + i])
                copy.start()
                copies.append(copy)
    for copy in copies:
        copy.wait()


def call(kernel, outs, scratch=(), scalars=0, work=(0, 0), inputs=0):
    vmem = pl.BlockSpec(memory_space=pltpu.VMEM)
    smem = pl.BlockSpec(memory_space=pltpu.SMEM)
    return pl.pallas_call(
        kernel,
        out_shape=[jax.ShapeDtypeStruct(s, jnp.float32) for s in outs],
        in_specs=[smem] * scalars + [vmem] * inputs,
        out_specs=[vmem] * len(outs),
        scratch_shapes=[pltpu.VMEM(s, jnp.float32) for s in scratch],
        cost_estimate=pl.CostEstimate(flops=work[0], bytes_accessed=work[1], transcendentals=0),
        compiler_params=pltpu.CompilerParams(vmem_limit_bytes=GRANT),
    )


def local_step(density, moments, shifts):
    local, pick, side, weigh, powers = [jnp.asarray(t) for t in tables()]
    height = PLANES * LANES
    facing = pl.pallas_call(
        edge_kernel,
        out_shape=jax.ShapeDtypeStruct((SLOTS, ROWS, WIDTH), jnp.float32),
        in_specs=[pl.BlockSpec(memory_space=pltpu.HBM)] * 2,
        out_specs=pl.BlockSpec(memory_space=pltpu.VMEM),
        scratch_shapes=[pltpu.SemaphoreType.DMA((VARS,))],
        compiler_params=pltpu.CompilerParams(vmem_limit_bytes=16 * 2**20),
    )(*[pltpu.with_memory_space_constraint(x, pltpu.HBM) for x in (density, moments)])
    across = lax.ppermute(facing, "axial", [(0, 1), (1, 0)])
    vmem = pl.BlockSpec(memory_space=pltpu.VMEM)
    smem = pl.BlockSpec(memory_space=pltpu.SMEM)
    halo = jax.ShapeDtypeStruct((PAIRS, ROWS, WIDTH), jnp.float32)
    inside, outside, cols, turns = pl.pallas_call(
        pack_kernel,
        out_shape=[
            halo,
            halo,
            jax.ShapeDtypeStruct((8, height), jnp.float32),
            jax.ShapeDtypeStruct((PIECE,), jnp.int32),
        ],
        in_specs=[smem, vmem, vmem, vmem],
        out_specs=[vmem, vmem, vmem, smem],
        scratch_shapes=[pltpu.VMEM((height, WIDTH), jnp.float32)],
        cost_estimate=pl.CostEstimate(flops=10**6, bytes_accessed=10**6, transcendentals=0),
        compiler_params=pltpu.CompilerParams(vmem_limit_bytes=GRANT),
    )(shifts, density, moments, pick)
    count_r = lax.axis_size("radial")
    pairs = [(i, i ^ 1) for i in range(count_r)]
    between = [(i, i - 1 if i % 2 == 0 else i + 1) for i in range(1, count_r - 1)]
    inside = lax.ppermute(inside, "radial", pairs)
    outside = lax.ppermute(outside, "radial", between)
    ring = [(i, (i + 1) % RING) for i in range(RING)]
    back = [(j, i) for i, j in ring]
    left = lax.ppermute(cols, "pitch", ring)
    right = lax.ppermute(cols, "pitch", back)
    whole = lax.all_to_all(across.reshape(RING, PIECE, ROWS, WIDTH), "pitch", 0, 0)
    res, upd, sums = call(
        main_kernel,
        [(height, WIDTH), (height, WIDTH), (8, height)],
        scratch=[(height, WIDTH), (height, WIDTH)],
        inputs=6,
        work=(10**8, 2 * 10**6),
    )(density, moments, inside, outside, local, pick)
    (send,) = call(
        align_kernel,
        [(RING * SENT, WIDTH)],
        scratch=[(2 * RING, ROWS, WIDTH), (RING * PIECE * ROWS, WIDTH)],
        scalars=1,
        inputs=4,
        work=(10**7, 10**6),
    )(turns, whole, sums, weigh, powers)
    send, left, right = lax.optimization_barrier((send, left, right))
    got = lax.all_to_all(send.reshape(RING, SENT // 4, 4, WIDTH), "pitch", 0, 0)
    got = got.reshape(RING * SENT, WIDTH)
    shape = (INST, VARS, PLANES, ROWS, WIDTH)
    held = pltpu.VMEM((PLANES, INST, VARS, ROWS, WIDTH), jnp.float32)
    return pl.pallas_call(
        final_kernel,
        out_shape=[jax.ShapeDtypeStruct(shape, jnp.float32)] * 2,
        in_specs=[pl.BlockSpec(memory_space=pltpu.VMEM)] * 7,
        out_specs=[pl.BlockSpec(memory_space=pl.ANY)] * 2,
        scratch_shapes=[held, held, pltpu.SemaphoreType.DMA((2 * PLANES,))],
        cost_estimate=pl.CostEstimate(flops=10**7, bytes_accessed=2 * 10**6, transcendentals=0),
        compiler_params=pltpu.CompilerParams(vmem_limit_bytes=GRANT),
    )(res, upd, got, left, right, local, side)


def solution(mesh):
    in_specs = (P(None, "axial", "radial", "pitch"), P(None, None, "axial", "radial", "pitch"), P())
    out_specs = (
        P(None, None, "axial", "radial", "pitch"),
        P(None, None, "axial", "radial", "pitch"),
    )
    return jax.shard_map(
        local_step, mesh=mesh, in_specs=in_specs, out_specs=out_specs, check_vma=False
    )
```

```python
import math

import jax
import jax.numpy as jnp
import numpy as np
from jax import lax
from jax.experimental import pallas as pl
from jax.experimental.pallas import tpu as pltpu
from jax.sharding import PartitionSpec as P


COEFFS = (0.75, -0.15, 1.0 / 60.0)
GAMMA_LESS = 0.4
HIGHEST = lax.Precision.HIGHEST

INST = 9
VARS = 5
PLANES = 2
ROWS = 8
WIDTH = 128
RING = 16
PAIRS = INST * VARS
PIECE = 3
SLOTS = RING * PIECE
LANES = SLOTS * ROWS
SENT = 36
GRANT = 16 * 2**20


def spectral_weights():
    return [0.5 * (-1.0) ** k / math.sin(math.pi * k / INST) for k in range(1, INST // 2 + 1)]


def tables():
    extent = WIDTH * RING
    eps = float(extent * extent // 16)
    rho = 2.0 * eps / (1.0 + 2.0 * eps + math.sqrt(1.0 + 4.0 * eps))
    gain = rho / (eps * (1.0 - rho * rho))
    lam = rho**WIDTH
    closing = 1.0 / (1.0 - lam**RING)
    at = np.arange(WIDTH)
    reach = np.zeros((WIDTH, WIDTH + 6))
    for k, weight in enumerate(COEFFS, 1):
        reach[at, at - k + 3] += weight
        reach[at, at + k + 3] -= weight
    spots = np.arange(-3, WIDTH + 3)
    green = gain * rho ** np.abs(at[:, None] - at[None, :])
    wide = gain * rho ** np.abs(spots[:, None] - at[None, :])
    local = np.concatenate([reach[:, 3:-3], reach @ wide, green], axis=1)
    rise = rho ** (WIDTH - 1.0 - at)
    fall = rho ** (at + 0.0)
    kappa = sum(weight * (rho**k - rho**-k) for k, weight in enumerate(COEFFS, 1))
    pick = np.zeros((16, WIDTH))
    pick[0:3, 0:3] = np.eye(3)
    pick[3:6, WIDTH - 3 :] = np.eye(3)
    pick[6] = kappa * rise
    pick[7] = -kappa * fall
    pick[8 + 6] = rise
    pick[8 + 7] = fall
    side = np.zeros((24, 2 * WIDTH))
    for c in range(3):
        for m in range(3):
            if 1 <= 3 + m - c <= 3:
                w = -COEFFS[3 + m - c - 1]
                side[3 + c, m] += w
                side[3 + c, WIDTH:] += w * gain * (rho ** np.abs(at - m) - rho ** (at - m + 0.0))
            if c + 1 + m <= 3:
                w = COEFFS[c + m]
                spot = WIDTH - 1 - m
                side[8 + c, spot] += w
                side[8 + c, WIDTH:] += w * gain * (
                    rho ** np.abs(at - spot) - rho ** (spot - at + 0.0)
                )
    side[16, WIDTH:] = gain * rho ** (at + 1.0)
    side[17, WIDTH:] = gain * rho ** (WIDTH - at + 0.0)
    sums = np.zeros((WIDTH, WIDTH))
    sums[:, 0:RING] = rise[:, None]
    sums[:, RING : 2 * RING] = fall[:, None]
    ring = np.arange(RING)
    powers = np.zeros((RING, WIDTH))
    powers[:, 0:RING] = closing * lam ** ((ring[None, :] - ring[:, None] - 1) % RING)
    powers[:, RING : 2 * RING] = closing * lam ** ((ring[:, None] - ring[None, :] - 1) % RING)
    return [np.asarray(t, np.float32) for t in (local, pick, side, sums, powers)]


def field(density, moments, v, a):
    return density[:, a] if v == 0 else moments[:, v - 1, a]


def dot(a, b, contract):
    return lax.dot_general(
        a, b, (contract, ((), ())), precision=HIGHEST, preferred_element_type=jnp.float32
    )


def split(a):
    high = a.astype(jnp.bfloat16)
    return high, (a - high.astype(jnp.float32)).astype(jnp.bfloat16)


def dot3(a, b, contract):
    (ah, al), (bh, bl) = split(a), split(b)

    def one(x, y):
        return lax.dot_general(x, y, (contract, ((), ())), preferred_element_type=jnp.float32)

    return one(ah, bh) + (one(ah, bl) + one(al, bh))


def row_index(shape):
    return lax.broadcasted_iota(jnp.int32, shape, len(shape) - 2)


def edge_kernel(density, moments, facing, sems):
    plane = 1 - lax.axis_index("axial")
    copies = []
    for v in range(VARS):
        source = density.at[:, plane] if v == 0 else moments.at[:, v - 1, plane]
        copies.append(
            pltpu.make_async_copy(source, facing.at[pl.ds(v * INST, INST)], sems.at[v])
        )
    for copy in copies:
        copy.start()
    facing[PAIRS:SLOTS] = jnp.zeros((SLOTS - PAIRS, ROWS, WIDTH), jnp.float32)
    for copy in copies:
        copy.wait()


def pack_kernel(density, moments, pick, inside, outside, cols, flux):
    even = lax.rem(lax.axis_index("radial"), 2) == 0
    low = row_index((INST, ROWS, WIDTH)) < 4
    for v in range(VARS):
        one, two = field(density, moments, v, 0), field(density, moments, v, 1)
        at = slice(v * INST, (v + 1) * INST)
        first = jnp.where(low, one, pltpu.roll(two, 4, 1))
        last = jnp.where(low, pltpu.roll(one, 4, 1), two)
        inside[at] = jnp.where(even, last, first)
        outside[at] = jnp.where(even, first, last)
    for a in range(PLANES):
        along = fluxes(*[field(density, moments, v, a) for v in range(VARS)], 2)
        put(flux, a, along)
    cols[...] = dot(pick[0:8], flux[...], ((1,), (1,)))


def put(ref, a, values):
    for v in range(VARS):
        at = (a * SLOTS + v * INST) * ROWS
        ref[at : at + INST * ROWS] = values[v].reshape(INST * ROWS, WIDTH)
    at = (a * SLOTS + PAIRS) * ROWS
    ref[at : (a + 1) * LANES] = jnp.zeros(((SLOTS - PAIRS) * ROWS, WIDTH), jnp.float32)


def fluxes(d, ma, mr, mp, e, dim):
    inverse = 1.0 / d
    pressure = GAMMA_LESS * (e - 0.5 * (ma * ma + mr * mr + mp * mp) * inverse)
    total = e + pressure
    if dim == 1:
        speed = mr * inverse
        return (mr, ma * speed, mr * speed + pressure, mp * speed, total * speed)
    speed = mp * inverse
    return (mp, ma * speed, mr * speed, mp * speed + pressure, total * speed)


def main_kernel(density, moments, inside, outside, local, pick, res, upd, sums, flux, rest):
    axial = lax.axis_index("axial")
    radial = lax.axis_index("radial")
    even = lax.rem(radial, 2) == 0
    shape = (INST, ROWS, WIDTH)
    row = row_index(shape)
    low = row < 4
    known = jnp.where(low, (radial < lax.axis_size("radial") - 1).astype(jnp.int32), (radial > 0).astype(jnp.int32)) > 0
    weights = spectral_weights()
    for a in range(PLANES):
        fields = [field(density, moments, v, a) for v in range(VARS)]
        rims = []
        for v in range(VARS):
            at = slice(v * INST, (v + 1) * INST)
            near, far = inside[at], outside[at]
            up, down = jnp.where(even, near, far), jnp.where(even, far, near)
            if a == 0:
                rims.append(jnp.where(low, up, pltpu.roll(down, 4, 1)))
            else:
                rims.append(jnp.where(low, pltpu.roll(up, 4, 1), down))
        along_radial, beyond = fluxes(*fields, 1), fluxes(*rims, 1)
        put(flux, a, fluxes(*fields, 2))
        added = []
        mask = jnp.where(axial == 0, a == PLANES - 1, a == 0).astype(jnp.float32)
        for v in range(VARS):
            own, rim = along_radial[v], jnp.where(known, beyond[v], 0.0)
            total = -mask * fields[v]
            for k, weight in enumerate(COEFFS, 1):
                ahead = pltpu.roll(jnp.where(row >= k, own, rim), ROWS - k, 1)
                behind = pltpu.roll(jnp.where(row < ROWS - k, own, rim), k, 1)
                total = total + weight * (ahead - behind)
            f = fields[v]
            for k, weight in enumerate(weights, 1):
                back = jnp.concatenate([f[INST - k :], f[: INST - k]], axis=0)
                forth = jnp.concatenate([f[k:], f[:k]], axis=0)
                total = total + weight * (back - forth)
            added.append(total)
        put(rest, a, added)
    through = dot3(flux[...], local[:, 0 : 2 * WIDTH], ((1,), (0,)))
    res[...] = rest[...] + through[:, 0:WIDTH]
    upd[...] = through[:, WIDTH:] + dot3(rest[...], local[:, 2 * WIDTH :], ((1,), (0,)))
    sums[...] = dot3(pick[0:8], flux[...], ((1,), (1,))) + dot3(
        pick[8:16], rest[...], ((1,), (1,))
    )


def turn_kernel(shifts, turns):
    axial, place = lax.axis_index("axial"), lax.axis_index("pitch")
    extent = WIDTH * RING
    for j in range(PIECE):
        shift = shifts[lax.rem(place * PIECE + j, INST)]
        turns[j] = jnp.where(axial == 1, shift, (extent - shift) & (extent - 1))


def align_kernel(turns, whole, sums, weigh, powers, out, rolled, kept):
    axial = lax.axis_index("axial")
    place = lax.axis_index("pitch")
    tall = PIECE * ROWS
    lane = lax.broadcasted_iota(jnp.int32, (ROWS, WIDTH), 1)
    for j in range(PIECE):
        blocks, within = turns[j] >> 7, turns[j] & (WIDTH - 1)
        turned = pltpu.roll(whole[:, j], within, 2)
        rolled[0:RING] = turned
        rolled[RING : 2 * RING] = turned
        for d in range(RING):
            here = rolled[RING + d - blocks]
            before = rolled[RING - 1 + d - blocks]
            window = jnp.where(lane < within, before, here)
            at = d * SENT + j * ROWS
            out[at : at + ROWS] = window
            at = d * tall + j * ROWS
            kept[at : at + ROWS] = window
    totals = dot3(kept[...], weigh[...], ((1,), (0,)))
    carried = totals[0:tall] * powers[0:1]
    for d in range(1, RING):
        carried = carried + totals[d * tall : (d + 1) * tall] * powers[d : d + 1]
    spread = powers[pl.ds(place, 1)]
    column = lax.broadcasted_iota(jnp.int32, (8, WIDTH), 1)
    line = row_index((8, WIDTH))
    extra = jnp.where(
        line == 0,
        jnp.where(column < RING, spread, 0.0),
        jnp.where((line == 1) & (column >= RING), spread, 0.0),
    )
    left = jnp.concatenate([carried, extra], axis=0)
    target = (1 - axial) * LANES + place * tall
    spots = lax.broadcasted_iota(jnp.int32, (tall, 2 * LANES), 1)
    select = (spots == target + row_index((tall, 2 * LANES))).astype(jnp.float32)
    right = jnp.concatenate([select, pltpu.roll(sums[...], 2, 0)], axis=0)
    carries = dot3(left[:, 0 : 2 * RING], right, ((0,), (0,)))
    for t in range(6):
        at = slice(t * WIDTH, (t + 1) * WIDTH)
        out[pl.ds(tall + t, RING, SENT)] = carries[0:RING, at]
        out[pl.ds(tall + 6 + t, RING, SENT)] = carries[RING : 2 * RING, at]


def final_kernel(res, upd, got, left, right, local, side, residual, update, first, second, sems):
    axial = lax.axis_index("axial")
    tall = PIECE * ROWS
    windows = jnp.concatenate([got[h * SENT : h * SENT + tall] for h in range(RING)], axis=0)
    smoothed = dot3(windows, local[:, 2 * WIDTH :], ((1,), (0,)))
    carries = got[tall:SENT]
    for h in range(1, RING):
        carries = carries + got[h * SENT + tall : (h + 1) * SENT]
    line = row_index((8, WIDTH))
    copies = []
    for t in range(6):
        a, part = t // 3, t % 3
        at = slice(t * WIDTH, (t + 1) * WIDTH)
        pair = jnp.where(
            line == 0, carries[t : t + 1], jnp.where(line == 1, carries[6 + t : 7 + t], 0.0)
        )
        sides = jnp.concatenate([left[:, at], right[:, at], pair], axis=0)
        added = dot3(sides, side[...], ((0,), (0,)))
        mine = axial == 1 - a
        here = slice(part * WIDTH, (part + 1) * WIDTH)
        r = res[at] + added[:, 0:WIDTH] + jnp.where(mine, windows[here], 0.0)
        u = upd[at] + added[:, WIDTH:] + jnp.where(mine, smoothed[here], 0.0)
        for j in range(16):
            pair_at = part * 16 + j
            if pair_at < PAIRS:
                v, n = pair_at // INST, pair_at % INST
                first[a, n, v] = r[j * ROWS : (j + 1) * ROWS]
                second[a, n, v] = u[j * ROWS : (j + 1) * ROWS]
        if part == 2:
            for i, (held, out) in enumerate(((first, residual), (second, update))):
                copy = pltpu.make_async_copy(held.at[a], out.at[:, :, a], sems.at[2 * a + i])
                copy.start()
                copies.append(copy)
    for copy in copies:
        copy.wait()


def call(kernel, outs, scratch=(), scalars=0, work=(0, 0), inputs=0):
    vmem = pl.BlockSpec(memory_space=pltpu.VMEM)
    smem = pl.BlockSpec(memory_space=pltpu.SMEM)
    return pl.pallas_call(
        kernel,
        out_shape=[jax.ShapeDtypeStruct(s, jnp.float32) for s in outs],
        in_specs=[smem] * scalars + [vmem] * inputs,
        out_specs=[vmem] * len(outs),
        scratch_shapes=[pltpu.VMEM(s, jnp.float32) for s in scratch],
        cost_estimate=pl.CostEstimate(flops=work[0], bytes_accessed=work[1], transcendentals=0),
        compiler_params=pltpu.CompilerParams(vmem_limit_bytes=GRANT),
    )


def local_step(density, moments, shifts):
    local, pick, side, weigh, powers = [jnp.asarray(t) for t in tables()]
    height = PLANES * LANES
    facing = pl.pallas_call(
        edge_kernel,
        out_shape=jax.ShapeDtypeStruct((SLOTS, ROWS, WIDTH), jnp.float32),
        in_specs=[pl.BlockSpec(memory_space=pltpu.HBM)] * 2,
        out_specs=pl.BlockSpec(memory_space=pltpu.VMEM),
        scratch_shapes=[pltpu.SemaphoreType.DMA((VARS,))],
        compiler_params=pltpu.CompilerParams(vmem_limit_bytes=16 * 2**20),
    )(*[pltpu.with_memory_space_constraint(x, pltpu.HBM) for x in (density, moments)])
    across = lax.ppermute(facing, "axial", [(0, 1), (1, 0)])
    vmem = pl.BlockSpec(memory_space=pltpu.VMEM)
    halo = jax.ShapeDtypeStruct((PAIRS, ROWS, WIDTH), jnp.float32)
    inside, outside, cols = pl.pallas_call(
        pack_kernel,
        out_shape=[
            halo,
            halo,
            jax.ShapeDtypeStruct((8, height), jnp.float32),
        ],
        in_specs=[vmem] * 3,
        out_specs=[vmem] * 3,
        scratch_shapes=[pltpu.VMEM((height, WIDTH), jnp.float32)],
        cost_estimate=pl.CostEstimate(flops=10**6, bytes_accessed=10**6, transcendentals=0),
        compiler_params=pltpu.CompilerParams(vmem_limit_bytes=GRANT),
    )(density, moments, pick)
    count_r = lax.axis_size("radial")
    pairs = [(i, i ^ 1) for i in range(count_r)]
    between = [(i, i - 1 if i % 2 == 0 else i + 1) for i in range(1, count_r - 1)]
    inside = lax.ppermute(inside, "radial", pairs)
    outside = lax.ppermute(outside, "radial", between)
    ring = [(i, (i + 1) % RING) for i in range(RING)]
    back = [(j, i) for i, j in ring]
    left = lax.ppermute(cols, "pitch", ring)
    right = lax.ppermute(cols, "pitch", back)
    whole = lax.all_to_all(across.reshape(RING, PIECE, ROWS, WIDTH), "pitch", 0, 0)
    res, upd, sums = call(
        main_kernel,
        [(height, WIDTH), (height, WIDTH), (8, height)],
        scratch=[(height, WIDTH), (height, WIDTH)],
        inputs=6,
        work=(10**8, 2 * 10**6),
    )(density, moments, inside, outside, local, pick)
    smem = pl.BlockSpec(memory_space=pltpu.SMEM)
    turns = pl.pallas_call(
        turn_kernel,
        out_shape=jax.ShapeDtypeStruct((PIECE,), jnp.int32),
        in_specs=[smem],
        out_specs=smem,
        compiler_params=pltpu.CompilerParams(vmem_limit_bytes=GRANT),
    )(shifts)
    (send,) = call(
        align_kernel,
        [(RING * SENT, WIDTH)],
        scratch=[(2 * RING, ROWS, WIDTH), (RING * PIECE * ROWS, WIDTH)],
        scalars=1,
        inputs=4,
        work=(10**7, 10**6),
    )(turns, whole, sums, weigh, powers)
    send, left, right = lax.optimization_barrier((send, left, right))
    got = lax.all_to_all(send.reshape(RING, SENT // 4, 4, WIDTH), "pitch", 0, 0)
    got = got.reshape(RING * SENT, WIDTH)
    shape = (INST, VARS, PLANES, ROWS, WIDTH)
    held = pltpu.VMEM((PLANES, INST, VARS, ROWS, WIDTH), jnp.float32)
    return pl.pallas_call(
        final_kernel,
        out_shape=[jax.ShapeDtypeStruct(shape, jnp.float32)] * 2,
        in_specs=[pl.BlockSpec(memory_space=pltpu.VMEM)] * 7,
        out_specs=[pl.BlockSpec(memory_space=pl.ANY)] * 2,
        scratch_shapes=[held, held, pltpu.SemaphoreType.DMA((2 * PLANES,))],
        cost_estimate=pl.CostEstimate(flops=10**7, bytes_accessed=2 * 10**6, transcendentals=0),
        compiler_params=pltpu.CompilerParams(vmem_limit_bytes=GRANT),
    )(res, upd, got, left, right, local, side)


def solution(mesh):
    in_specs = (P(None, "axial", "radial", "pitch"), P(None, None, "axial", "radial", "pitch"), P())
    out_specs = (
        P(None, None, "axial", "radial", "pitch"),
        P(None, None, "axial", "radial", "pitch"),
    )
    return jax.shard_map(
        local_step, mesh=mesh, in_specs=in_specs, out_specs=out_specs, check_vma=False
    )
```

```python
import math

import jax
import jax.numpy as jnp
import numpy as np
from jax import lax
from jax.experimental import pallas as pl
from jax.experimental.pallas import tpu as pltpu
from jax.sharding import PartitionSpec as P


COEFFS = (0.75, -0.15, 1.0 / 60.0)
GAMMA_LESS = 0.4
HIGHEST = lax.Precision.HIGHEST

INST = 9
VARS = 5
PLANES = 2
ROWS = 8
WIDTH = 128
RING = 16
PAIRS = INST * VARS
PIECE = 3
SLOTS = RING * PIECE
LANES = SLOTS * ROWS
SENT = 36
GRANT = 16 * 2**20


def spectral_weights():
    return [0.5 * (-1.0) ** k / math.sin(math.pi * k / INST) for k in range(1, INST // 2 + 1)]


def tables():
    extent = WIDTH * RING
    eps = float(extent * extent // 16)
    rho = 2.0 * eps / (1.0 + 2.0 * eps + math.sqrt(1.0 + 4.0 * eps))
    gain = rho / (eps * (1.0 - rho * rho))
    lam = rho**WIDTH
    closing = 1.0 / (1.0 - lam**RING)
    at = np.arange(WIDTH)
    reach = np.zeros((WIDTH, WIDTH + 6))
    for k, weight in enumerate(COEFFS, 1):
        reach[at, at - k + 3] += weight
        reach[at, at + k + 3] -= weight
    spots = np.arange(-3, WIDTH + 3)
    green = gain * rho ** np.abs(at[:, None] - at[None, :])
    wide = gain * rho ** np.abs(spots[:, None] - at[None, :])
    local = np.concatenate([reach[:, 3:-3], reach @ wide, green], axis=1)
    rise = rho ** (WIDTH - 1.0 - at)
    fall = rho ** (at + 0.0)
    kappa = sum(weight * (rho**k - rho**-k) for k, weight in enumerate(COEFFS, 1))
    pick = np.zeros((16, WIDTH))
    pick[0:3, 0:3] = np.eye(3)
    pick[3:6, WIDTH - 3 :] = np.eye(3)
    pick[6] = kappa * rise
    pick[7] = -kappa * fall
    pick[8 + 6] = rise
    pick[8 + 7] = fall
    side = np.zeros((24, 2 * WIDTH))
    for c in range(3):
        for m in range(3):
            if 1 <= 3 + m - c <= 3:
                w = -COEFFS[3 + m - c - 1]
                side[3 + c, m] += w
                side[3 + c, WIDTH:] += w * gain * (rho ** np.abs(at - m) - rho ** (at - m + 0.0))
            if c + 1 + m <= 3:
                w = COEFFS[c + m]
                spot = WIDTH - 1 - m
                side[8 + c, spot] += w
                side[8 + c, WIDTH:] += w * gain * (
                    rho ** np.abs(at - spot) - rho ** (spot - at + 0.0)
                )
    side[16, WIDTH:] = gain * rho ** (at + 1.0)
    side[17, WIDTH:] = gain * rho ** (WIDTH - at + 0.0)
    sums = np.zeros((WIDTH, WIDTH))
    sums[:, 0:RING] = rise[:, None]
    sums[:, RING : 2 * RING] = fall[:, None]
    ring = np.arange(RING)
    powers = np.zeros((RING, WIDTH))
    powers[:, 0:RING] = closing * lam ** ((ring[None, :] - ring[:, None] - 1) % RING)
    powers[:, RING : 2 * RING] = closing * lam ** ((ring[:, None] - ring[None, :] - 1) % RING)
    return [np.asarray(t, np.float32) for t in (local, pick, side, sums, powers)]


def field(density, moments, v, a):
    return density[:, a] if v == 0 else moments[:, v - 1, a]


def dot(a, b, contract):
    return lax.dot_general(
        a, b, (contract, ((), ())), precision=HIGHEST, preferred_element_type=jnp.float32
    )


def split(a):
    high = a.astype(jnp.bfloat16)
    return high, (a - high.astype(jnp.float32)).astype(jnp.bfloat16)


def dot3(a, b, contract):
    (ah, al), (bh, bl) = split(a), split(b)

    def one(x, y):
        return lax.dot_general(x, y, (contract, ((), ())), preferred_element_type=jnp.float32)

    return one(ah, bh) + (one(ah, bl) + one(al, bh))


def row_index(shape):
    return lax.broadcasted_iota(jnp.int32, shape, len(shape) - 2)


def edge_kernel(density, moments, facing, sems):
    plane = 1 - lax.axis_index("axial")
    copies = []
    for v in range(VARS):
        source = density.at[:, plane] if v == 0 else moments.at[:, v - 1, plane]
        copies.append(
            pltpu.make_async_copy(source, facing.at[pl.ds(v * INST, INST)], sems.at[v])
        )
    for copy in copies:
        copy.start()
    facing[PAIRS:SLOTS] = jnp.zeros((SLOTS - PAIRS, ROWS, WIDTH), jnp.float32)
    for copy in copies:
        copy.wait()


def pack_kernel(shifts, density, moments, pick, inside, outside, cols, turns, flux):
    axial, place = lax.axis_index("axial"), lax.axis_index("pitch")
    extent = WIDTH * RING
    for j in range(PIECE):
        shift = shifts[lax.rem(place * PIECE + j, INST)]
        turns[j] = jnp.where(axial == 1, shift, (extent - shift) & (extent - 1))
    even = lax.rem(lax.axis_index("radial"), 2) == 0
    low = row_index((INST, ROWS, WIDTH)) < 4
    for v in range(VARS):
        one, two = field(density, moments, v, 0), field(density, moments, v, 1)
        at = slice(v * INST, (v + 1) * INST)
        first = jnp.where(low, one, pltpu.roll(two, 4, 1))
        last = jnp.where(low, pltpu.roll(one, 4, 1), two)
        inside[at] = jnp.where(even, last, first)
        outside[at] = jnp.where(even, first, last)
    for a in range(PLANES):
        along = fluxes(*[field(density, moments, v, a) for v in range(VARS)], 2)
        put(flux, a, along)
    cols[...] = dot(pick[0:8], flux[...], ((1,), (1,)))


def put(ref, a, values):
    for v in range(VARS):
        at = (a * SLOTS + v * INST) * ROWS
        ref[at : at + INST * ROWS] = values[v].reshape(INST * ROWS, WIDTH)
    at = (a * SLOTS + PAIRS) * ROWS
    ref[at : (a + 1) * LANES] = jnp.zeros(((SLOTS - PAIRS) * ROWS, WIDTH), jnp.float32)


def fluxes(d, ma, mr, mp, e, dim):
    inverse = 1.0 / d
    pressure = GAMMA_LESS * (e - 0.5 * (ma * ma + mr * mr + mp * mp) * inverse)
    total = e + pressure
    if dim == 1:
        speed = mr * inverse
        return (mr, ma * speed, mr * speed + pressure, mp * speed, total * speed)
    speed = mp * inverse
    return (mp, ma * speed, mr * speed, mp * speed + pressure, total * speed)


def main_kernel(density, moments, inside, outside, local, pick, res, upd, sums, flux, rest):
    axial = lax.axis_index("axial")
    radial = lax.axis_index("radial")
    even = lax.rem(radial, 2) == 0
    shape = (INST, ROWS, WIDTH)
    row = row_index(shape)
    low = row < 4
    known = jnp.where(low, (radial < lax.axis_size("radial") - 1).astype(jnp.int32), (radial > 0).astype(jnp.int32)) > 0
    weights = spectral_weights()
    for a in range(PLANES):
        fields = [field(density, moments, v, a) for v in range(VARS)]
        rims = []
        for v in range(VARS):
            at = slice(v * INST, (v + 1) * INST)
            near, far = inside[at], outside[at]
            up, down = jnp.where(even, near, far), jnp.where(even, far, near)
            if a == 0:
                rims.append(jnp.where(low, up, pltpu.roll(down, 4, 1)))
            else:
                rims.append(jnp.where(low, pltpu.roll(up, 4, 1), down))
        along_radial, beyond = fluxes(*fields, 1), fluxes(*rims, 1)
        put(flux, a, fluxes(*fields, 2))
        added = []
        mask = jnp.where(axial == 0, a == PLANES - 1, a == 0).astype(jnp.float32)
        for v in range(VARS):
            own, rim = along_radial[v], jnp.where(known, beyond[v], 0.0)
            total = -mask * fields[v]
            for k, weight in enumerate(COEFFS, 1):
                ahead = pltpu.roll(jnp.where(row >= k, own, rim), ROWS - k, 1)
                behind = pltpu.roll(jnp.where(row < ROWS - k, own, rim), k, 1)
                total = total + weight * (ahead - behind)
            f = fields[v]
            for k, weight in enumerate(weights, 1):
                back = jnp.concatenate([f[INST - k :], f[: INST - k]], axis=0)
                forth = jnp.concatenate([f[k:], f[:k]], axis=0)
                total = total + weight * (back - forth)
            added.append(total)
        put(rest, a, added)
    through = dot(flux[...], local[:, 0 : 2 * WIDTH], ((1,), (0,)))
    res[...] = rest[...] + through[:, 0:WIDTH]
    upd[...] = through[:, WIDTH:] + dot(rest[...], local[:, 2 * WIDTH :], ((1,), (0,)))
    sums[...] = dot(pick[0:8], flux[...], ((1,), (1,))) + dot(
        pick[8:16], rest[...], ((1,), (1,))
    )


def align_kernel(turns, whole, sums, weigh, powers, out, rolled, kept):
    axial = lax.axis_index("axial")
    place = lax.axis_index("pitch")
    tall = PIECE * ROWS
    lane = lax.broadcasted_iota(jnp.int32, (ROWS, WIDTH), 1)
    for j in range(PIECE):
        blocks, within = turns[j] >> 7, turns[j] & (WIDTH - 1)
        turned = pltpu.roll(whole[:, j], within, 2)
        rolled[0:RING] = turned
        rolled[RING : 2 * RING] = turned
        for d in range(RING):
            here = rolled[RING + d - blocks]
            before = rolled[RING - 1 + d - blocks]
            window = jnp.where(lane < within, before, here)
            at = d * SENT + j * ROWS
            out[at : at + ROWS] = window
            at = d * tall + j * ROWS
            kept[at : at + ROWS] = window
    totals = dot3(kept[...], weigh[...], ((1,), (0,)))
    carried = totals[0:tall] * powers[0:1]
    for d in range(1, RING):
        carried = carried + totals[d * tall : (d + 1) * tall] * powers[d : d + 1]
    spread = powers[pl.ds(place, 1)]
    column = lax.broadcasted_iota(jnp.int32, (8, WIDTH), 1)
    line = row_index((8, WIDTH))
    extra = jnp.where(
        line == 0,
        jnp.where(column < RING, spread, 0.0),
        jnp.where((line == 1) & (column >= RING), spread, 0.0),
    )
    left = jnp.concatenate([carried, extra], axis=0)
    target = (1 - axial) * LANES + place * tall
    spots = lax.broadcasted_iota(jnp.int32, (tall, 2 * LANES), 1)
    select = (spots == target + row_index((tall, 2 * LANES))).astype(jnp.float32)
    right = jnp.concatenate([select, pltpu.roll(sums[...], 2, 0)], axis=0)
    carries = dot3(left[:, 0 : 2 * RING], right, ((0,), (0,)))
    for t in range(6):
        at = slice(t * WIDTH, (t + 1) * WIDTH)
        out[pl.ds(tall + t, RING, SENT)] = carries[0:RING, at]
        out[pl.ds(tall + 6 + t, RING, SENT)] = carries[RING : 2 * RING, at]


def final_kernel(res, upd, got, left, right, local, side, residual, update, first, second, sems):
    axial = lax.axis_index("axial")
    tall = PIECE * ROWS
    windows = jnp.concatenate([got[h * SENT : h * SENT + tall] for h in range(RING)], axis=0)
    smoothed = dot3(windows, local[:, 2 * WIDTH :], ((1,), (0,)))
    carries = got[tall:SENT]
    for h in range(1, RING):
        carries = carries + got[h * SENT + tall : (h + 1) * SENT]
    line = row_index((8, WIDTH))
    pair = jnp.concatenate(
        [
            jnp.where(
                line == 0, carries[t : t + 1], jnp.where(line == 1, carries[6 + t : 7 + t], 0.0)
            )
            for t in range(6)
        ],
        axis=1,
    )
    sides = jnp.concatenate([left[...], right[...], pair], axis=0)
    whole = dot3(sides, side[...], ((0,), (0,)))
    copies = []
    for t in range(6):
        a, part = t // 3, t % 3
        at = slice(t * WIDTH, (t + 1) * WIDTH)
        added = whole[at]
        mine = axial == 1 - a
        here = slice(part * WIDTH, (part + 1) * WIDTH)
        r = res[at] + added[:, 0:WIDTH] + jnp.where(mine, windows[here], 0.0)
        u = upd[at] + added[:, WIDTH:] + jnp.where(mine, smoothed[here], 0.0)
        for j in range(16):
            pair_at = part * 16 + j
            if pair_at < PAIRS:
                v, n = pair_at // INST, pair_at % INST
                first[a, n, v] = r[j * ROWS : (j + 1) * ROWS]
                second[a, n, v] = u[j * ROWS : (j + 1) * ROWS]
        if part == 2:
            for i, (held, out) in enumerate(((first, residual), (second, update))):
                copy = pltpu.make_async_copy(held.at[a], out.at[:, :, a], sems.at[2 * a + i])
                copy.start()
                copies.append(copy)
    for copy in copies:
        copy.wait()


def call(kernel, outs, scratch=(), scalars=0, work=(0, 0), inputs=0):
    vmem = pl.BlockSpec(memory_space=pltpu.VMEM)
    smem = pl.BlockSpec(memory_space=pltpu.SMEM)
    return pl.pallas_call(
        kernel,
        out_shape=[jax.ShapeDtypeStruct(s, jnp.float32) for s in outs],
        in_specs=[smem] * scalars + [vmem] * inputs,
        out_specs=[vmem] * len(outs),
        scratch_shapes=[pltpu.VMEM(s, jnp.float32) for s in scratch],
        cost_estimate=pl.CostEstimate(flops=work[0], bytes_accessed=work[1], transcendentals=0),
        compiler_params=pltpu.CompilerParams(vmem_limit_bytes=GRANT),
    )


def local_step(density, moments, shifts):
    local, pick, side, weigh, powers = [jnp.asarray(t) for t in tables()]
    height = PLANES * LANES
    facing = pl.pallas_call(
        edge_kernel,
        out_shape=jax.ShapeDtypeStruct((SLOTS, ROWS, WIDTH), jnp.float32),
        in_specs=[pl.BlockSpec(memory_space=pltpu.HBM)] * 2,
        out_specs=pl.BlockSpec(memory_space=pltpu.VMEM),
        scratch_shapes=[pltpu.SemaphoreType.DMA((VARS,))],
        compiler_params=pltpu.CompilerParams(vmem_limit_bytes=16 * 2**20),
    )(*[pltpu.with_memory_space_constraint(x, pltpu.HBM) for x in (density, moments)])
    across = lax.ppermute(facing, "axial", [(0, 1), (1, 0)])
    vmem = pl.BlockSpec(memory_space=pltpu.VMEM)
    smem = pl.BlockSpec(memory_space=pltpu.SMEM)
    halo = jax.ShapeDtypeStruct((PAIRS, ROWS, WIDTH), jnp.float32)
    inside, outside, cols, turns = pl.pallas_call(
        pack_kernel,
        out_shape=[
            halo,
            halo,
            jax.ShapeDtypeStruct((8, height), jnp.float32),
            jax.ShapeDtypeStruct((PIECE,), jnp.int32),
        ],
        in_specs=[smem, vmem, vmem, vmem],
        out_specs=[vmem, vmem, vmem, smem],
        scratch_shapes=[pltpu.VMEM((height, WIDTH), jnp.float32)],
        cost_estimate=pl.CostEstimate(flops=10**6, bytes_accessed=10**6, transcendentals=0),
        compiler_params=pltpu.CompilerParams(vmem_limit_bytes=GRANT),
    )(shifts, density, moments, pick)
    count_r = lax.axis_size("radial")
    pairs = [(i, i ^ 1) for i in range(count_r)]
    between = [(i, i - 1 if i % 2 == 0 else i + 1) for i in range(1, count_r - 1)]
    inside = lax.ppermute(inside, "radial", pairs)
    outside = lax.ppermute(outside, "radial", between)
    ring = [(i, (i + 1) % RING) for i in range(RING)]
    back = [(j, i) for i, j in ring]
    left = lax.ppermute(cols, "pitch", ring)
    right = lax.ppermute(cols, "pitch", back)
    whole = lax.all_to_all(across.reshape(RING, PIECE, ROWS, WIDTH), "pitch", 0, 0)
    res, upd, sums = call(
        main_kernel,
        [(height, WIDTH), (height, WIDTH), (8, height)],
        scratch=[(height, WIDTH), (height, WIDTH)],
        inputs=6,
        work=(10**8, 2 * 10**6),
    )(density, moments, inside, outside, local, pick)
    (send,) = call(
        align_kernel,
        [(RING * SENT, WIDTH)],
        scratch=[(2 * RING, ROWS, WIDTH), (RING * PIECE * ROWS, WIDTH)],
        scalars=1,
        inputs=4,
        work=(10**7, 10**6),
    )(turns, whole, sums, weigh, powers)
    send, left, right = lax.optimization_barrier((send, left, right))
    got = lax.all_to_all(send.reshape(RING, SENT // 4, 4, WIDTH), "pitch", 0, 0)
    got = got.reshape(RING * SENT, WIDTH)
    shape = (INST, VARS, PLANES, ROWS, WIDTH)
    held = pltpu.VMEM((PLANES, INST, VARS, ROWS, WIDTH), jnp.float32)
    return pl.pallas_call(
        final_kernel,
        out_shape=[jax.ShapeDtypeStruct(shape, jnp.float32)] * 2,
        in_specs=[pl.BlockSpec(memory_space=pltpu.VMEM)] * 7,
        out_specs=[pl.BlockSpec(memory_space=pl.ANY)] * 2,
        scratch_shapes=[held, held, pltpu.SemaphoreType.DMA((2 * PLANES,))],
        cost_estimate=pl.CostEstimate(flops=10**7, bytes_accessed=2 * 10**6, transcendentals=0),
        compiler_params=pltpu.CompilerParams(vmem_limit_bytes=GRANT),
    )(res, upd, got, left, right, local, side)


def solution(mesh):
    in_specs = (P(None, "axial", "radial", "pitch"), P(None, None, "axial", "radial", "pitch"), P())
    out_specs = (
        P(None, None, "axial", "radial", "pitch"),
        P(None, None, "axial", "radial", "pitch"),
    )
    return jax.shard_map(
        local_step, mesh=mesh, in_specs=in_specs, out_specs=out_specs, check_vma=False
    )
```
